32 devices in a mesh: tok: 8 (over z, y), vocab: 4 (over x, core).
Axes of the slice: x: 2, y: 2, z: 4, core: 2. Of those that a mesh axis runs over, the one named last changes fastest.
Arguments:
- hidden: bfloat16 [12288, 2048], P('tok')
- gain: float32 [2048], replicated, may hold values from 0.1 to 1.9
- head: bfloat16 [16384, 2048], P(('tok', 'vocab'))
- targets: int32 [12288], P('tok'), may hold values from 0 to 16383
- lengths: int32 [64], P('tok'), may hold values from 1 to 383, as said below
- group_map: int32 [64, 1], P('tok'), may hold values from 0 to 7
Outputs:
- logprob: float32 [12288], P(('tok', 'vocab'))
- entropy: float32 [12288], P(('tok', 'vocab'))
- centered: float32 [64], P(('tok', 'vocab'))
The draws below stay inside these ranges and needn't reach their ends.
Inputs may be any that keep to these rules, and one draw needn't show every extreme that they name: `lengths`: the 8 requests of one index of tok hold 960 + e tokens in all and those of the index half the axis away hold 960 - e, for some e from 0 to 576; some index holds exactly 1536. `group_map`: every group number names one or more requests.
All inputs are finite; a program needn't handle non-finite values.
Results may differ from the reference program's by a relative error of at most 0.0003.
The reference program's roundings to bfloat16 on the way (of `normed`) count: a program that leaves them out, or rounds other values in their place, can miss the bound.
Values may be sent and summed in bfloat16 or wider, within the bound.
No kernel may reach another device: no remote copies, remote signals or barrier semaphores. Data moves between devices by JAX's collectives and lax.ppermute only.
A program may use at most 128 MiB of HBM per device.

```python
import math
import jax
import jax.numpy as jnp
import numpy as np
from jax import lax

D = 2048
V = 16384
CAP = 1536
LIVE = 960
REQ_DEV = 8
TOKENS = 12288
REQS = 64
GROUPS = 8
N_TOK = 8


def hot_layout(key):
    hot_rows = jax.random.permutation(jax.random.fold_in(key, 111), V)[:8].astype(jnp.int32)
    signs = (jax.random.randint(jax.random.fold_in(key, 112), (4, 8), 0, 2) * 2 - 1).astype(jnp.float32)
    patterns = signs / math.sqrt(8.0)
    strengths = jnp.array([130.0, 220.0, 310.0, 400.0], jnp.float32)
    return (hot_rows, patterns, strengths)


def shared_head(key):
    weights = jax.random.normal(jax.random.fold_in(key, 101), (V, D), jnp.float32) * (3.0 / math.sqrt(D))
    hot_rows, patterns, strengths = hot_layout(key)
    pair_index = jnp.arange(8) // 2
    offsets = 2.0 * (jnp.arange(8) % 2).astype(jnp.float32)
    hot_values = patterns[pair_index] * (strengths[pair_index] - offsets)[:, None]
    full_rows = jnp.concatenate([hot_values, jnp.zeros((8, D - 8), jnp.float32)], axis=1)
    match = (jnp.arange(V)[:, None] == hot_rows[None, :]).astype(jnp.float32)
    replaced = jnp.sum(match[:, :, None] * full_rows[None, :, :], axis=1)
    is_hot = jnp.sum(match, axis=1, keepdims=True) > 0.5
    return jnp.where(is_hot, replaced, weights)


def draw_head(key, part):
    return shared_head(key).astype(jnp.bfloat16)


def draw_hidden(key, part):
    base_key = jax.random.fold_in(key, 201)
    states = jax.random.normal(base_key, (TOKENS, D), jnp.float32)
    reserved = (jnp.arange(D) < 8)[None, :]
    states = jnp.where(reserved, 0.0, states)
    hot_rows, patterns, strengths = hot_layout(key)
    pair_choice = jax.random.randint(jax.random.fold_in(key, 203), (TOKENS,), 0, 4)
    strength = jnp.exp(jax.random.uniform(jax.random.fold_in(key, 204), (TOKENS, 1), jnp.float32) * math.log(4.0))
    aligned = jnp.concatenate([patterns[pair_choice], jnp.zeros((TOKENS, D - 8), jnp.float32)], axis=1) * strength
    slot_position = jnp.arange(TOKENS) % CAP
    selected = ((slot_position == 1) | (slot_position == 3))[:, None]
    states = jnp.where(selected, aligned, states)
    return states.astype(jnp.bfloat16)


def draw_lengths(key, part):
    device_count = REQS // REQ_DEV
    half_count = device_count // 2
    spare = CAP - LIVE
    excess = jax.random.randint(jax.random.fold_in(key, 301), (half_count,), 0, spare + 1)
    fullest = jax.random.randint(jax.random.fold_in(key, 302), (), 0, half_count)
    excess = jnp.where(jnp.arange(half_count) == fullest, spare, excess)
    direction = jax.random.randint(jax.random.fold_in(key, 303), (half_count,), 0, 2) * 2 - 1
    device_loads = jnp.concatenate([LIVE + direction * excess, LIVE - direction * excess])
    quotient = device_loads // REQ_DEV
    remainder = device_loads % REQ_DEV
    position = jnp.arange(REQ_DEV)
    base_lengths = quotient[:, None] + (position[None, :] < remainder[:, None]).astype(jnp.int32)
    moved = jax.random.randint(jax.random.fold_in(key, 304), (device_count, REQ_DEV // 2), 0, quotient[:, None])
    fullest_sign = jnp.sum(jnp.where(jnp.arange(half_count) == fullest, direction, 0))
    fullest_device = jnp.where(fullest_sign > 0, fullest, fullest + half_count)
    pinned = (jnp.arange(device_count)[:, None] == fullest_device) & (jnp.arange(REQ_DEV // 2)[None, :] == 0)
    moved = jnp.where(pinned, quotient[:, None] - 1, moved)
    shifts = jnp.stack([moved, -moved], axis=-1).reshape(device_count, REQ_DEV)
    return (base_lengths + shifts).reshape(-1).astype(jnp.int32)


def place_ends(values, own_key, least, largest):
    index_at = [jax.random.randint(jax.random.fold_in(own_key, axis), (), 0, length) for axis, length in enumerate(values.shape)]
    longest = values.shape.index(max(values.shape))
    next_to = index_at[:longest] + [(index_at[longest] + 1) % values.shape[longest]] + index_at[longest + 1:]
    return values.at[tuple(index_at)].set(least).at[tuple(next_to)].set(largest)


def rank_table(count, lean):
    portions = [(1 << 20) // math.isqrt(rank ** lean) + 1 for rank in range(1, count + 1)]
    width = 1 + sum(portions) // (1 << 30)
    return np.cumsum(np.array([max(1, weight // width) for weight in portions]))


def skewed_ids(key, dims, count, lean):
    listing = rank_table(count, lean)
    pick = jax.random.randint(jax.random.fold_in(key, 1), dims, 0, int(listing[count - 1]))
    standing = jnp.searchsorted(jnp.asarray(listing, jnp.int32), pick, side="right")
    return jax.random.permutation(jax.random.fold_in(key, 2), count)[standing].astype(jnp.int32)


def choose_distinct(stream_key, rows, number_of, top, lift):
    order = jax.random.permutation(jax.random.fold_in(stream_key, 1), number_of)
    pull = order
    for power in range(3):
        pull = pull * pull // number_of
    pull = pull * lift // number_of
    lots = jax.random.randint(jax.random.fold_in(stream_key, 2), (rows, number_of), 0, 4096) + pull
    holders = jax.random.permutation(jax.random.fold_in(stream_key, 3), rows)[jnp.arange(number_of) % rows]
    lots = jnp.where(jnp.arange(rows)[:, None] == holders[None, :], 1 << 14, lots)
    score = lots * number_of + jnp.arange(number_of)
    return lax.top_k(score.astype(jnp.int32), top)[1].astype(jnp.int32)


def setup_inputs(seed: int = 0) -> dict:
    key_of = jax.random.split(jax.random.key(seed), 7)
    return {
        "hidden": draw_hidden(jax.random.fold_in(key_of[6], 71), 0),
        "gain": jnp.clip(1.0 + 0.18 * jax.random.normal(key_of[1], (D,), jnp.float32), 0.1, 1.9),
        "head": draw_head(jax.random.fold_in(key_of[6], 71), 0),
        "targets": place_ends(skewed_ids(key_of[3], (TOKENS,), V, 2), jax.random.fold_in(key_of[3], 3), 0, V - 1).astype(jnp.int32),
        "lengths": draw_lengths(jax.random.fold_in(key_of[6], 71), 0),
        "group_map": choose_distinct(key_of[5], REQS, GROUPS, 1, 1024),
    }


EPS = 1e-06

def normalize(states, gain):
    values = states.astype(jnp.float32)
    scale_inv = lax.rsqrt(lax.optimization_barrier(jnp.mean(values * values, axis=-1, keepdims=True)) + EPS)
    return (values * scale_inv * gain.astype(jnp.float32)[None, :]).astype(jnp.bfloat16)

def reference(hidden, gain, head, targets, lengths, group_map):
    feature_count = hidden.shape[1]
    per_device = lengths.reshape(N_TOK, REQ_DEV)
    device_loads = lax.optimization_barrier(jnp.sum(per_device, axis=1))
    slot_index = jnp.arange(CAP, dtype=jnp.int32)

    def score_block(inputs):
        states, wanted, own_load = inputs
        normed = normalize(states, gain)
        logits = jnp.dot(normed, head.T, preferred_element_type=jnp.float32)
        highest = lax.optimization_barrier(jnp.max(logits, axis=1))
        exponent = jnp.exp(logits - highest[:, None])
        exp_total = lax.optimization_barrier(jnp.sum(exponent, axis=1))
        moment = lax.optimization_barrier(jnp.sum(exponent * logits, axis=1))
        log_total = highest + jnp.log(exp_total)
        picked = jnp.take_along_axis(logits, wanted[:, None], axis=1)[:, 0]
        is_live = slot_index < own_load
        return (jnp.where(is_live, picked - log_total, 0.0), jnp.where(is_live, log_total - moment / exp_total, 0.0))
    logprob, entropy = lax.map(score_block, (hidden.reshape(N_TOK, CAP, feature_count), targets.reshape(N_TOK, CAP), device_loads))
    finish = jnp.cumsum(per_device, axis=1)
    starts = finish - per_device
    member = ((slot_index[None, :, None] >= starts[:, None, :]) & (slot_index[None, :, None] < finish[:, None, :])).astype(jnp.float32)
    request_sums = lax.optimization_barrier(jnp.sum(member * logprob[:, :, None], axis=1))
    mean_logprob = (request_sums / per_device.astype(jnp.float32)).reshape(-1)
    onehot = (group_map[:, 0][:, None] == jnp.arange(GROUPS, dtype=jnp.int32)[None, :]).astype(jnp.float32)
    group_sums = lax.optimization_barrier(jnp.sum(onehot * mean_logprob[:, None], axis=0))
    counts = lax.optimization_barrier(jnp.sum(onehot, axis=0))
    group_mean = group_sums / counts
    centered = mean_logprob - lax.optimization_barrier(jnp.sum(onehot * group_mean[None, :], axis=1))
    return (logprob.reshape(-1), entropy.reshape(-1), centered)
```

```python
import functools

import jax
import jax.numpy as jnp
from jax import lax
from jax.experimental import pallas as pl
from jax.experimental.pallas import tpu as pltpu
from jax.sharding import PartitionSpec as P

EPS = 1e-06
LOW = -1e30
BOTH = ("tok", "vocab")
TOK, VOCAB, NZ, NY = 8, 4, 4, 2


def combined_all(value, axis, join):
    pieces = jax.tree.map(lambda part: lax.all_gather(part, axis), value)
    head = jax.tree.map(lambda part: part[0], pieces)
    tail = jax.tree.map(lambda part: part[1:], pieces)
    so_far, _ = lax.scan(lambda so_far, piece: (join(so_far, piece), None), head, tail)
    return so_far


def normalize(states, gain):
    values = states.astype(jnp.float32)
    scale_inv = lax.rsqrt(jnp.mean(values * values, axis=-1, keepdims=True) + EPS)
    return (values * scale_inv * gain).astype(jnp.bfloat16)


def combine(left_part, right_part):
    highest = jnp.maximum(left_part[0], right_part[0])
    left_scale = jnp.exp(left_part[0] - highest)
    right_scale = jnp.exp(right_part[0] - highest)
    return (
        highest,
        left_part[1] * left_scale + right_part[1] * right_scale,
        left_part[2] * left_scale + right_part[2] * right_scale,
        left_part[3] + right_part[3],
    )


def score(states, wanted, gain, head):
    normed = normalize(states, gain[None, :])
    logits = jnp.einsum(
        "nd,vd->nv",
        normed,
        lax.all_gather(head, "tok", axis=0, tiled=True),
        preferred_element_type=jnp.float32,
    )
    vocab_block = head.shape[0]
    vocab_shards = lax.axis_size("vocab")
    shard_index = lax.axis_index("vocab")
    owned = wanted // vocab_block % vocab_shards == shard_index
    column = wanted // (vocab_block * vocab_shards) * vocab_block + wanted % vocab_block
    column = jnp.where(owned, column, -1)
    columns = lax.broadcasted_iota(jnp.int32, logits.shape, 1)
    highest = jnp.max(logits, axis=1)
    exponent = jnp.exp(logits - highest[:, None])
    exp_total = jnp.sum(exponent, axis=1)
    moment = jnp.sum(exponent * logits, axis=1)
    picked = jnp.sum(jnp.where(columns == column[:, None], logits, 0.0), axis=1)
    highest, exp_total, moment, picked = combined_all(
        (highest, exp_total, moment, picked), "vocab", combine
    )
    log_total = highest + jnp.log(exp_total)
    return (picked - log_total, log_total - moment / exp_total)


def on_any_mesh(hidden, gain, head, targets, lengths, group_map):
    capacity = hidden.shape[0]
    own_load = jnp.sum(lengths)
    slot_index = jnp.arange(capacity, dtype=jnp.int32)
    logprob, entropy = score(hidden, targets, gain, head)
    is_live = slot_index < own_load
    logprob = jnp.where(is_live, logprob, 0.0)
    entropy = jnp.where(is_live, entropy, 0.0)
    finish = jnp.cumsum(lengths)
    starts = finish - lengths
    member = (
        (slot_index[:, None] >= starts[None, :]) & (slot_index[:, None] < finish[None, :])
    ).astype(jnp.float32)
    request_sums = jnp.sum(member * logprob[:, None], axis=0)
    mean_logprob = request_sums / lengths.astype(jnp.float32)
    groups_count = lengths.shape[0] * lax.axis_size("tok") // 8
    onehot = (
        group_map[:, 0][:, None] == jnp.arange(groups_count, dtype=jnp.int32)[None, :]
    ).astype(jnp.float32)
    group_sums, counts = lax.psum(
        (jnp.sum(onehot * mean_logprob[:, None], axis=0), jnp.sum(onehot, axis=0)), "tok"
    )
    group_mean = group_sums / counts
    centered = mean_logprob - jnp.sum(onehot * group_mean[None, :], axis=1)
    vocab_shards = lax.axis_size("vocab")
    shard_index = lax.axis_index("vocab")
    slot_share = capacity // vocab_shards
    request_share = lengths.shape[0] // vocab_shards
    return (
        lax.dynamic_slice_in_dim(logprob, shard_index * slot_share, slot_share, 0),
        lax.dynamic_slice_in_dim(entropy, shard_index * slot_share, slot_share, 0),
        lax.dynamic_slice_in_dim(centered, shard_index * request_share, request_share, 0),
    )


def device_pairs(target):
    pairs = []
    for z in range(NZ):
        for y in range(NY):
            for x in range(2):
                for c in range(2):
                    to = target(z, y, x, c)
                    if to is not None:
                        pairs.append(
                            ((z * NY + y) * VOCAB + x * 2 + c, (to[0] * NY + to[1]) * VOCAB + to[2] * 2 + to[3])
                        )
    return pairs


def send(value, target):
    return lax.ppermute(value, BOTH, device_pairs(target))


def to_x(value):
    return send(value, lambda z, y, x, c: (z, y, 1 - x, c))


def to_y(value):
    return send(value, lambda z, y, x, c: (z, 1 - y, x, c))


def to_core(value):
    return send(value, lambda z, y, x, c: (z, y, x, 1 - c))


def to_partner(value):
    return send(value, lambda z, y, x, c: (z ^ 2, y, x, c))


def round_z(value, step):
    return send(value, lambda z, y, x, c: ((z + step) % NZ, y, x, c))


def up(value, first):
    return send(value, lambda z, y, x, c: (z + 1, y, x, c) if first <= z < NZ - 1 else None)


def down(value, first):
    return send(value, lambda z, y, x, c: (z - 1, y, x, c) if 0 < z <= NZ - 1 - first else None)


SHARE = 384
EVEN = 240
SURE = 96
REST = EVEN - SURE
PIECE = 256


def prep_kernel(which, h0, h1, h2, h3, gain_ref, sure_ref, rest_ref, trade_ref):
    gain = gain_ref[...]
    row = lax.broadcasted_iota(jnp.int32, (SURE, SURE), 0)
    col = lax.broadcasted_iota(jnp.int32, (SURE, SURE), 1)
    mirror = (row + col == SURE - 1).astype(jnp.bfloat16)

    def flip(block):
        return jnp.dot(mirror, block, preferred_element_type=jnp.float32).astype(jnp.bfloat16)

    sure_ref[...] = normalize(h0[...], gain)
    rest_ref[0:SURE, :] = normalize(h1[...], gain)
    third = normalize(h2[...], gain)
    rest_ref[SURE:REST, :] = third[0 : REST - SURE, :]
    trade_ref[0:SURE, :] = flip(normalize(h3[...], gain))
    trade_ref[SURE:REST, :] = flip(third)[0 : REST - SURE, :]


def prepare(hidden, gain, quarter):
    width = hidden.shape[1]

    def block(j):
        return pl.BlockSpec((SURE, width), lambda i, which, j=j: (VOCAB * j + which[0], 0))

    def whole(rows):
        return pl.BlockSpec((rows, width), lambda i, which: (0, 0))

    return pl.pallas_call(
        prep_kernel,
        grid_spec=pltpu.PrefetchScalarGridSpec(
            num_scalar_prefetch=1,
            grid=(1,),
            in_specs=[block(j) for j in range(4)] + [whole(1)],
            out_specs=[whole(SURE), whole(REST), whole(REST)],
        ),
        out_shape=[jax.ShapeDtypeStruct((n, width), jnp.bfloat16) for n in (SURE, REST, REST)],
        cost_estimate=pl.CostEstimate(flops=4 * 10**8, bytes_accessed=3 * 10**6, transcendentals=SHARE),
        name="prep",
    )(quarter.reshape(1), hidden, hidden, hidden, hidden, gain[None, :])


def stats_kernel(plan, n_pieces, n_tok_refs, head_plan, scalars, tgt_ref, *refs):
    tok_refs = refs[:n_tok_refs]
    n_head_refs = 1 + max(index for index, _ in head_plan)
    head_refs = refs[n_tok_refs : n_tok_refs + n_head_refs]
    out_ref, tok_buf, head_buf, logit_buf, state, tok_sem, head_sem = refs[n_tok_refs + n_head_refs :]
    tokens = tok_buf.shape[0]
    z = scalars[0]
    for piece, (index, start) in enumerate(head_plan):
        pltpu.make_async_copy(
            head_refs[index].at[pl.ds(start, PIECE)],
            head_buf.at[pl.ds(piece * PIECE, PIECE)],
            head_sem.at[piece],
        ).start()
    for at in range(NZ):

        @pl.when(z == at)
        def _():
            for seg, (index, offset) in enumerate(plan[at]):
                ref = tok_refs[index]
                pltpu.make_async_copy(
                    ref, tok_buf.at[pl.ds(offset, ref.shape[0])], tok_sem.at[seg]
                ).start()

    for seg, (index, offset) in enumerate(plan[0]):
        ref = tok_refs[index]
        pltpu.make_async_copy(ref, tok_buf.at[pl.ds(offset, ref.shape[0])], tok_sem.at[seg]).wait()
    state[0] = jnp.full((8, tokens), LOW, jnp.float32)
    for k in range(1, 4):
        state[k] = jnp.zeros((8, tokens), jnp.float32)
    group = 2 * PIECE
    chunk = 32 if tokens > 300 else 64

    def part(row):
        return logit_buf[row : row + chunk, :].reshape(chunk // 8, 8, tokens)

    rows = lax.broadcasted_iota(jnp.int32, (chunk // 8, 8, tokens), 0) * 8 + lax.broadcasted_iota(
        jnp.int32, (chunk // 8, 8, tokens), 1
    )

    def body(g, carry):
        for half in range(2):
            pltpu.make_async_copy(
                head_refs[0].at[pl.ds(0, PIECE)],
                head_buf.at[pl.ds(g * group + half * PIECE, PIECE)],
                head_sem.at[2 * g + half],
            ).wait()
        logit_buf[...] = lax.dot_general(
            head_buf[pl.ds(g * group, group), :],
            tok_buf[...],
            (((1,), (1,)), ((), ())),
            preferred_element_type=jnp.float32,
        )
        top_before = state[0]
        top = top_before
        for row in range(0, group, chunk):
            top = jnp.maximum(top, jnp.max(part(row), axis=0))
        shift = top_before - top
        scale = jnp.exp(shift)
        total = state[1] * scale
        moment = (state[2] + shift * state[1]) * scale
        picked = state[3]
        for half in range(2):
            wanted = tgt_ref[...] - scalars[1 + 2 * g + half]
            for row in range(0, PIECE, chunk):
                logits = part(half * PIECE + row)
                under = logits - top[None]
                weight = jnp.exp(under)
                total += jnp.sum(weight, axis=0)
                moment += jnp.sum(weight * under, axis=0)
                picked += jnp.sum(
                    jnp.where(rows == (wanted - row)[None], logits, 0.0), axis=0
                )
        state[0] = top
        state[1] = total
        state[2] = moment
        state[3] = picked
        return carry

    lax.fori_loop(0, n_pieces // 2, body, 0)
    top8 = state[0]
    top = jnp.max(top8, axis=0, keepdims=True)
    shift = top8 - top
    scale = jnp.exp(shift)
    out_ref[0:1, :] = top
    out_ref[1:2, :] = jnp.sum(state[1] * scale, axis=0, keepdims=True)
    out_ref[2:3, :] = jnp.sum((state[2] + shift * state[1]) * scale, axis=0, keepdims=True)
    out_ref[3:4, :] = jnp.sum(state[3], axis=0, keepdims=True)
    out_ref[4:8, :] = jnp.zeros((4, tokens), jnp.float32)


def statistics(name, z, wanted, tok_refs, plan, heads):
    tokens = wanted.shape[1]
    arrays, head_plan = [], []
    for array, start, _ in heads:
        for index, known in enumerate(arrays):
            if known is array:
                break
        else:
            index = len(arrays)
            arrays.append(array)
        head_plan.append((index, start))
    scalars = jnp.stack([z] + [base for _, _, base in heads]).astype(jnp.int32)
    width = arrays[0].shape[1]
    n_pieces = len(heads)
    vocab = n_pieces * PIECE
    return pl.pallas_call(
        functools.partial(stats_kernel, plan, n_pieces, len(tok_refs), head_plan),
        grid_spec=pltpu.PrefetchScalarGridSpec(
            num_scalar_prefetch=1,
            grid=(1,),
            in_specs=[pl.BlockSpec((1, tokens), lambda i, s: (0, 0))]
            + [pl.BlockSpec(memory_space=pl.ANY)] * (len(tok_refs) + len(arrays)),
            out_specs=pl.BlockSpec((8, tokens), lambda i, s: (0, 0)),
            scratch_shapes=[
                pltpu.VMEM((tokens, width), jnp.bfloat16),
                pltpu.VMEM((vocab, width), jnp.bfloat16),
                pltpu.VMEM((2 * PIECE, tokens), jnp.float32),
                pltpu.VMEM((4, 8, tokens), jnp.float32),
                pltpu.SemaphoreType.DMA((len(plan[0]),)),
                pltpu.SemaphoreType.DMA((n_pieces,)),
            ],
        ),
        out_shape=jax.ShapeDtypeStruct((8, tokens), jnp.float32),
        compiler_params=pltpu.CompilerParams(vmem_limit_bytes=32 * 1024 * 1024),
        cost_estimate=pl.CostEstimate(
            flops=2 * tokens * vocab * width,
            bytes_accessed=2 * (tokens + vocab) * width,
            transcendentals=tokens * vocab,
        ),
        name=name,
    )(scalars, wanted, *tok_refs, *arrays)


def join(parts):
    top = functools.reduce(jnp.maximum, [part[0] for part in parts])
    total = moment = picked = 0.0
    for part in parts:
        shift = part[0] - top
        scale = jnp.exp(shift)
        total += part[1] * scale
        moment += (part[2] + shift * part[1]) * scale
        picked += part[3]
    return top, total, moment, picked


def on_device(hidden, gain, head, targets, lengths, group_map):
    tok = lax.axis_index("tok")
    vocab = lax.axis_index("vocab")
    z, y = tok // NY, tok % NY
    x, core = vocab // 2, vocab % 2
    upper = z >= NZ // 2
    quarter = jnp.where(upper, VOCAB - 1 - vocab, vocab)

    sure, rest_own, trade = prepare(hidden, gain, quarter)
    traded = to_partner(trade)
    load = jnp.sum(lengths)
    block_start = (jnp.arange(4) * VOCAB + quarter) * SURE
    live = jnp.sum(jnp.clip(load - block_start, 0, SURE))
    slot = lax.broadcasted_iota(jnp.int32, (REST, 1), 0) + SURE
    rest = jnp.where(slot < live, rest_own, traded)

    def line(value):
        ups, downs = [value], [value]
        for first in range(NZ - 1):
            ups.append(up(ups[-1], first))
            downs.append(down(downs[-1], first))
        return ups, downs

    sure_up, sure_down = line(sure)
    rest_up, rest_down = line(rest)

    own_small = jnp.concatenate(
        [
            lax.dynamic_index_in_dim(targets.reshape(4, VOCAB, SURE), quarter, 1, False).reshape(-1),
            lengths,
            group_map[:, 0],
            jnp.zeros((112,), jnp.int32),
        ]
    )
    turned = jnp.stack([own_small] + [round_z(own_small, step) for step in (1, 2, 3)])
    source = (z - jnp.arange(NZ)) % NZ
    small = jnp.sum(
        jnp.where((source[None, :] == jnp.arange(NZ)[:, None])[:, :, None], turned[None], 0), axis=1
    )
    tgt = small[:, :SHARE]
    meta_own = small[:, SHARE : SHARE + 16]
    meta_other = to_y(meta_own)
    meta = jnp.where(y == 0, jnp.stack([meta_own, meta_other], 1), jnp.stack([meta_other, meta_own], 1))
    all_lengths, all_groups = meta[:, :, :8], meta[:, :, 8:]

    zs = jnp.arange(NZ)
    loads = jnp.sum(meta_own[:, :8], axis=1)
    quarters = jnp.where(zs >= NZ // 2, VOCAB - 1 - vocab, vocab)
    starts_of = (jnp.arange(4)[None, :] * VOCAB + quarters[:, None]) * SURE
    lives = jnp.sum(jnp.clip(loads[:, None] - starts_of, 0, SURE), axis=1)
    slots = jnp.arange(EVEN)
    stays = slots[None, :] < lives[:, None]
    partner = jnp.array([2, 3, 0, 1])
    tgt_back = jnp.flip(jnp.concatenate([tgt[2:], tgt[:2]], 0)[:, SHARE - REST :], 1)
    tgt_even = jnp.where(
        stays, tgt[:, :EVEN], jnp.concatenate([tgt[:, :SURE], tgt_back], 1)
    ) - z * (TOK * VOCAB // NZ * head.shape[0])
    tgt_sure = tgt_even[:, :SURE].reshape(1, NZ * SURE)
    tgt_rest = tgt_even[:, SURE:]
    tgt_near = jnp.where(upper, tgt_rest[2:], tgt_rest[:2]).reshape(1, 2 * REST)
    tgt_mid = jnp.where(upper, tgt_rest[1:2], tgt_rest[2:3])
    tgt_far = jnp.where(upper, tgt_rest[0:1], tgt_rest[3:4])

    low_half, high_half = head[:PIECE], head[PIECE:]
    xa, ya = to_x(low_half), to_y(high_half)
    xb, yb = to_x(high_half), to_y(low_half)
    x2, y2 = to_x(ya), to_y(xa)

    def base(at_y, at_x, at_core, half):
        return ((at_y * 2 + at_x) * 2 + at_core) * (2 * PIECE) + half * PIECE

    def both_cores(piece, at_y, at_x, half):
        return [
            (piece, 0, base(at_y, at_x, core, half)),
            (to_core(piece), 0, base(at_y, at_x, 1 - core, half)),
        ]

    head_core = to_core(head)
    heads_own = [
        (array, half * PIECE, base(y, x, at_core, half))
        for array, at_core in ((head, core), (head_core, 1 - core))
        for half in range(2)
    ]
    heads_a = heads_own + both_cores(xa, y, 1 - x, 0) + both_cores(ya, 1 - y, x, 1)
    heads_b = both_cores(xb, y, 1 - x, 1) + both_cores(yb, 1 - y, x, 0)
    heads_c = both_cores(x2, 1 - y, 1 - x, 1) + both_cores(y2, 1 - y, 1 - x, 0)

    def from_set(at, of):
        return at - of if of <= at else 3 + of - at

    sure_refs = sure_up + sure_down[1:]
    rest_refs = rest_up + rest_down[1:]
    plan_sure = [[(from_set(at, of), of * SURE) for of in range(NZ)] for at in range(NZ)]
    plan_near = [[(from_set(at, at // 2 * 2 + k), k * REST) for k in range(2)] for at in range(NZ)]
    plan_mid = [[(from_set(at, 2 if at < 2 else 1), 0)] for at in range(NZ)]
    plan_far = [[(from_set(at, 3 if at < 2 else 0), 0)] for at in range(NZ)]

    def compact(refs, plan):
        used = sorted({index for rows in plan for index, _ in rows})
        return [refs[index] for index in used], [
            [(used.index(index), offset) for index, offset in rows] for rows in plan
        ]

    near_refs, plan_near = compact(rest_refs, plan_near)
    mid_refs, plan_mid = compact(rest_refs, plan_mid)
    far_refs, plan_far = compact(rest_refs, plan_far)
    sure_1 = statistics("sure_ab", z, tgt_sure, sure_refs, plan_sure, heads_a + heads_b)
    near_1 = statistics("near_ab", z, tgt_near, near_refs, plan_near, heads_a + heads_b)
    plan_c = [
        a + [(index + len(sure_refs), offset + NZ * SURE) for index, offset in b]
        for a, b in zip(plan_sure, plan_near)
    ]
    both_2 = statistics(
        "early_c", z, jnp.concatenate([tgt_sure, tgt_near], 1), sure_refs + near_refs, plan_c, heads_c
    )
    mid = statistics("mid", z, tgt_mid, mid_refs, plan_mid, heads_a + heads_b + heads_c)
    far = statistics("far", z, tgt_far, far_refs, plan_far, heads_a + heads_b + heads_c)

    sure_all = jnp.stack(join([sure_1, both_2[:, : NZ * SURE]])).reshape(4, NZ, SURE)
    near_all = jnp.stack(join([near_1, both_2[:, NZ * SURE :]])).reshape(4, 2, REST)
    mid, far = mid[:4, None], far[:4, None]
    rest_all = jnp.where(
        upper,
        jnp.concatenate([far, mid, near_all], 1),
        jnp.concatenate([near_all, mid, far], 1),
    )
    own_stats = jnp.concatenate([sure_all, rest_all], 2)
    top, total, moment, picked = join([own_stats] + [round_z(own_stats, step) for step in (1, 2, 3)])
    spread = jnp.log(total)
    logprob = picked - top - spread
    entropy = spread - moment / total

    local = jnp.where(stays, slots[None, :], 2 * EVEN - 1 - slots[None, :])
    origin = jnp.where(stays, zs[:, None], partner[:, None])
    origin_quarter = jnp.where(origin >= NZ // 2, VOCAB - 1 - vocab, vocab)
    row = (local // SURE * VOCAB + origin_quarter) * SURE + local % SURE
    place = origin * hidden.shape[0] + row
    finish = jnp.cumsum(meta_own[:, :8], axis=1) + zs[:, None] * hidden.shape[0]
    begin = finish - meta_own[:, :8]
    member = (place[:, :, None, None] >= begin) & (place[:, :, None, None] < finish)
    sums_part = jnp.sum(jnp.where(member, logprob[:, :, None, None], 0.0), axis=(0, 1))

    results = jnp.stack([logprob, entropy])
    mine = lax.dynamic_index_in_dim(results, z, 1, False)
    theirs = lax.dynamic_index_in_dim(results, z ^ 2, 1, False)
    local_rows = jnp.concatenate([mine, jnp.flip(theirs[:, SURE:], 1)], 1)
    local_rows = jnp.where(jnp.arange(SHARE)[None, :] < live, local_rows, 0.0)
    gathered = lax.all_gather(
        jnp.concatenate([local_rows.reshape(1, -1), sums_part.reshape(1, -1)], 1), "vocab"
    ).reshape(VOCAB, -1)
    sums_own = jnp.sum(gathered[:, 2 * SHARE :], axis=0)
    sums_other = to_y(sums_own)
    sums = jnp.where(
        y == 0, jnp.stack([sums_own, sums_other]), jnp.stack([sums_other, sums_own])
    ).reshape(NY, NZ, 8).transpose(1, 0, 2)
    parts = gathered[:, : 2 * SHARE].reshape(VOCAB, 2, SHARE)
    parts = lax.dynamic_slice_in_dim(parts, vocab * SURE, SURE, 2)
    parts = jnp.where(upper, jnp.flip(parts, 0), parts)
    out = parts.transpose(1, 0, 2).reshape(2, SHARE)

    means = (sums / all_lengths.astype(jnp.float32)).reshape(-1)
    onehot = (
        all_groups.reshape(-1)[:, None] == jnp.arange(TOK, dtype=jnp.int32)[None, :]
    ).astype(jnp.float32)
    group_mean = jnp.sum(onehot * means[:, None], axis=0) / jnp.sum(onehot, axis=0)
    centered = means - jnp.sum(onehot * group_mean[None, :], axis=1)
    return out[0], out[1], lax.dynamic_slice_in_dim(centered, tok * 8 + vocab * 2, 2, 0)


def solution(mesh):
    fits = mesh.shape["tok"] == TOK and mesh.shape["vocab"] == VOCAB
    return jax.shard_map(
        on_device if fits else on_any_mesh,
        mesh=mesh,
        in_specs=(
            P("tok", None),
            P(),
            P(("tok", "vocab"), None),
            P("tok"),
            P("tok"),
            P("tok", None),
        ),
        out_specs=(P(("tok", "vocab")), P(("tok", "vocab")), P(("tok", "vocab"))),
        check_vma=False,
    )
```

```python
import functools

import jax
import jax.numpy as jnp
from jax import lax
from jax.experimental import pallas as pl
from jax.experimental.pallas import tpu as pltpu
from jax.sharding import PartitionSpec as P

EPS = 1e-06
LOW = -1e30
BOTH = ("tok", "vocab")
TOK, VOCAB, NZ, NY = 8, 4, 4, 2


def combined_all(value, axis, join):
    pieces = jax.tree.map(lambda part: lax.all_gather(part, axis), value)
    head = jax.tree.map(lambda part: part[0], pieces)
    tail = jax.tree.map(lambda part: part[1:], pieces)
    so_far, _ = lax.scan(lambda so_far, piece: (join(so_far, piece), None), head, tail)
    return so_far


def normalize(states, gain):
    values = states.astype(jnp.float32)
    scale_inv = lax.rsqrt(jnp.mean(values * values, axis=-1, keepdims=True) + EPS)
    return (values * scale_inv * gain).astype(jnp.bfloat16)


def combine(left_part, right_part):
    highest = jnp.maximum(left_part[0], right_part[0])
    left_scale = jnp.exp(left_part[0] - highest)
    right_scale = jnp.exp(right_part[0] - highest)
    return (
        highest,
        left_part[1] * left_scale + right_part[1] * right_scale,
        left_part[2] * left_scale + right_part[2] * right_scale,
        left_part[3] + right_part[3],
    )


def score(states, wanted, gain, head):
    normed = normalize(states, gain[None, :])
    logits = jnp.einsum(
        "nd,vd->nv",
        normed,
        lax.all_gather(head, "tok", axis=0, tiled=True),
        preferred_element_type=jnp.float32,
    )
    vocab_block = head.shape[0]
    vocab_shards = lax.axis_size("vocab")
    shard_index = lax.axis_index("vocab")
    owned = wanted // vocab_block % vocab_shards == shard_index
    column = wanted // (vocab_block * vocab_shards) * vocab_block + wanted % vocab_block
    column = jnp.where(owned, column, -1)
    columns = lax.broadcasted_iota(jnp.int32, logits.shape, 1)
    highest = jnp.max(logits, axis=1)
    exponent = jnp.exp(logits - highest[:, None])
    exp_total = jnp.sum(exponent, axis=1)
    moment = jnp.sum(exponent * logits, axis=1)
    picked = jnp.sum(jnp.where(columns == column[:, None], logits, 0.0), axis=1)
    highest, exp_total, moment, picked = combined_all(
        (highest, exp_total, moment, picked), "vocab", combine
    )
    log_total = highest + jnp.log(exp_total)
    return (picked - log_total, log_total - moment / exp_total)


def on_any_mesh(hidden, gain, head, targets, lengths, group_map):
    capacity = hidden.shape[0]
    own_load = jnp.sum(lengths)
    slot_index = jnp.arange(capacity, dtype=jnp.int32)
    logprob, entropy = score(hidden, targets, gain, head)
    is_live = slot_index < own_load
    logprob = jnp.where(is_live, logprob, 0.0)
    entropy = jnp.where(is_live, entropy, 0.0)
    finish = jnp.cumsum(lengths)
    starts = finish - lengths
    member = (
        (slot_index[:, None] >= starts[None, :]) & (slot_index[:, None] < finish[None, :])
    ).astype(jnp.float32)
    request_sums = jnp.sum(member * logprob[:, None], axis=0)
    mean_logprob = request_sums / lengths.astype(jnp.float32)
    groups_count = lengths.shape[0] * lax.axis_size("tok") // 8
    onehot = (
        group_map[:, 0][:, None] == jnp.arange(groups_count, dtype=jnp.int32)[None, :]
    ).astype(jnp.float32)
    group_sums, counts = lax.psum(
        (jnp.sum(onehot * mean_logprob[:, None], axis=0), jnp.sum(onehot, axis=0)), "tok"
    )
    group_mean = group_sums / counts
    centered = mean_logprob - jnp.sum(onehot * group_mean[None, :], axis=1)
    vocab_shards = lax.axis_size("vocab")
    shard_index = lax.axis_index("vocab")
    slot_share = capacity // vocab_shards
    request_share = lengths.shape[0] // vocab_shards
    return (
        lax.dynamic_slice_in_dim(logprob, shard_index * slot_share, slot_share, 0),
        lax.dynamic_slice_in_dim(entropy, shard_index * slot_share, slot_share, 0),
        lax.dynamic_slice_in_dim(centered, shard_index * request_share, request_share, 0),
    )


def device_pairs(target):
    pairs = []
    for z in range(NZ):
        for y in range(NY):
            for x in range(2):
                for c in range(2):
                    to = target(z, y, x, c)
                    if to is not None:
                        pairs.append(
                            ((z * NY + y) * VOCAB + x * 2 + c, (to[0] * NY + to[1]) * VOCAB + to[2] * 2 + to[3])
                        )
    return pairs


def send(value, target):
    return lax.ppermute(value, BOTH, device_pairs(target))


def to_x(value):
    return send(value, lambda z, y, x, c: (z, y, 1 - x, c))


def to_y(value):
    return send(value, lambda z, y, x, c: (z, 1 - y, x, c))


def to_core(value):
    return send(value, lambda z, y, x, c: (z, y, x, 1 - c))


def across(value, step):
    return send(value, lambda z, y, x, c: (z ^ step, y, x, c))


SHARE = 384
EVEN = 240
SURE = 96
REST = EVEN - SURE
TILE = 256
NOTES = TILE - EVEN
PIECE = 256
GROUP = 2 * PIECE


def prep_kernel(which, h0, h1, h2, h3, gain_ref, tgt_ref, sure_ref, own_ref, trade_ref):
    gain = gain_ref[...]
    slots_count = tgt_ref.shape[1]
    row = lax.broadcasted_iota(jnp.int32, (SURE, SURE), 0)
    col = lax.broadcasted_iota(jnp.int32, (SURE, SURE), 1)
    mirror = (row + col == SURE - 1).astype(jnp.bfloat16)

    def flip(block):
        return jnp.dot(mirror, block, preferred_element_type=jnp.float32).astype(jnp.bfloat16)

    sure_ref[...] = normalize(h0[...], gain)
    own_ref[0:SURE, :] = normalize(h1[...], gain)
    third = normalize(h2[...], gain)
    own_ref[SURE:REST, :] = third[0 : REST - SURE, :]
    trade_ref[0:SURE, :] = flip(normalize(h3[...], gain))
    trade_ref[SURE:REST, :] = flip(third)[0 : REST - SURE, :]

    wanted = tgt_ref[...]
    level = lax.broadcasted_iota(jnp.int32, (NOTES, slots_count), 0)
    digits = jnp.where(level == 0, wanted & 127, jnp.where(level == 1, wanted >> 7, 0))
    digits = digits.astype(jnp.float32).astype(jnp.bfloat16)
    source = lax.broadcasted_iota(jnp.int32, (slots_count, TILE), 0)
    lane = lax.broadcasted_iota(jnp.int32, (1, TILE), 1)

    def notes(local, keep):
        block = (
            (local >= SURE).astype(jnp.int32)
            + (local >= 2 * SURE).astype(jnp.int32)
            + (local >= 3 * SURE).astype(jnp.int32)
        )
        at = local + block * ((VOCAB - 1) * SURE) + which[0] * SURE
        at = jnp.where(keep, at, -1)
        pick = jnp.where(source == at, 1.0, 0.0).astype(jnp.bfloat16)
        return jnp.dot(digits, pick, preferred_element_type=jnp.float32).astype(jnp.bfloat16)

    own_ref[REST : REST + NOTES, :] = jnp.zeros((NOTES, own_ref.shape[1]), jnp.bfloat16)
    own_ref[REST : REST + NOTES, 0:TILE] = notes(lane, lane < EVEN)
    trade_ref[REST : REST + NOTES, :] = jnp.zeros((NOTES, own_ref.shape[1]), jnp.bfloat16)
    trade_ref[REST : REST + NOTES, 0:TILE] = notes(
        2 * EVEN - 1 - lane, (lane >= SURE) & (lane < EVEN)
    )


def prepare(hidden, gain, targets, quarter):
    width = hidden.shape[1]

    def block(j):
        return pl.BlockSpec((SURE, width), lambda i, which, j=j: (VOCAB * j + which[0], 0))

    def whole(*shape):
        return pl.BlockSpec(shape, lambda i, which: (0, 0))

    return pl.pallas_call(
        prep_kernel,
        grid_spec=pltpu.PrefetchScalarGridSpec(
            num_scalar_prefetch=1,
            grid=(1,),
            in_specs=[block(j) for j in range(4)] + [whole(1, width), whole(1, targets.shape[0])],
            out_specs=[whole(n, width) for n in (SURE, REST + NOTES, REST + NOTES)],
        ),
        out_shape=[
            jax.ShapeDtypeStruct((n, width), jnp.bfloat16) for n in (SURE, REST + NOTES, REST + NOTES)
        ],
        cost_estimate=pl.CostEstimate(flops=4 * 10**8, bytes_accessed=3 * 10**6, transcendentals=SHARE),
        name="prep",
    )(quarter.reshape(1), hidden, hidden, hidden, hidden, gain[None, :], targets[None, :])


def merge_kernel(live_ref, own_ref, traded_ref, sizes_ref, out_ref):
    live = live_ref[0]
    for low in range(0, REST, 48):
        slot = lax.broadcasted_iota(jnp.int32, (48, own_ref.shape[1]), 0) + (SURE + low)
        out_ref[low : low + 48, :] = jnp.where(
            slot < live,
            own_ref[low : low + 48, :].astype(jnp.float32),
            traded_ref[low : low + 48, :].astype(jnp.float32),
        ).astype(jnp.bfloat16)
    lane = lax.broadcasted_iota(jnp.int32, (NOTES, TILE), 1)
    out_ref[REST : REST + NOTES, :] = jnp.zeros((NOTES, own_ref.shape[1]), jnp.bfloat16)
    out_ref[REST : REST + NOTES, 0:TILE] = (
        jnp.where(
            lane < live,
            own_ref[REST : REST + NOTES, 0:TILE].astype(jnp.float32),
            traded_ref[REST : REST + NOTES, 0:TILE].astype(jnp.float32),
        )
        + sizes_ref[...]
    ).astype(jnp.bfloat16)


def merge(live, own, traded, sizes):
    def whole(array):
        return pl.BlockSpec(array.shape, lambda i, s: (0, 0))

    return pl.pallas_call(
        merge_kernel,
        grid_spec=pltpu.PrefetchScalarGridSpec(
            num_scalar_prefetch=1,
            grid=(1,),
            in_specs=[whole(own), whole(traded), whole(sizes)],
            out_specs=whole(own),
        ),
        out_shape=jax.ShapeDtypeStruct(own.shape, own.dtype),
        cost_estimate=pl.CostEstimate(flops=10**6, bytes_accessed=3 * 10**6, transcendentals=0),
        name="merge",
    )(live.reshape(1), own, traded, sizes)


def stats_kernel(units, n_sets, n_known, final, head_plan, scalars, *refs):
    known_ref = refs[0] if n_known else None
    refs = refs[1:] if n_known else refs
    tok_refs = refs[: 2 * n_sets]
    n_head_refs = 1 + max(index for index, _ in head_plan)
    head_refs = refs[2 * n_sets : 2 * n_sets + n_head_refs]
    (out_ref, tok_buf, head_buf, logit_buf, state, wanted_buf, tok_sem, head_sem) = refs[
        2 * n_sets + n_head_refs :
    ]
    n_groups = len(head_plan) // 2
    n_units = len(units)
    at_set, at_group, at_base = 2, 2 + n_units + 1, 2 + 2 * (n_units + 1)
    z, offset = scalars[0], scalars[1]
    lanes = (8, TILE)

    def fetch(g):
        for piece in (2 * g, 2 * g + 1):
            index, start = head_plan[piece]
            pltpu.make_async_copy(
                head_refs[index].at[pl.ds(start, PIECE)],
                head_buf.at[pl.ds(piece * PIECE, PIECE)],
                head_sem.at[piece],
            ).start()

    def tok_copy(half):
        return pltpu.make_async_copy(
            tok_refs[half],
            tok_buf.at[half // 2, pl.ds(SURE * (half % 2), tok_refs[half].shape[0])],
            tok_sem.at[half],
        )

    for half in range(2 * n_sets):
        tok_copy(half).start()
    for g in range(min(2, n_groups)):
        fetch(g)
    logit_buf[...] = jnp.full(logit_buf.shape, LOW, jnp.float32)
    for k in range(n_sets):
        state[k, 0] = jnp.full(lanes, LOW, jnp.float32)
        for row in range(1, 4):
            state[k, row] = jnp.zeros(lanes, jnp.float32)
    if not final:
        for k in range(n_known):
            for row in range(4):
                state[k, row, 0:1, :] = known_ref[k, row : row + 1, :]
    notes = []
    for k in range(n_sets):
        tok_copy(2 * k).wait()
        tok_copy(2 * k + 1).wait()
        digits = tok_buf[k, EVEN:TILE, 0:TILE].astype(jnp.float32)
        wanted_buf[k] = (digits[0:1, :] + 128.0 * digits[1:2, :]).astype(jnp.int32) - offset
        notes.append(digits[2:3, :] + 128.0 * digits[3:4, :])
    chunk = 64
    rows = lax.broadcasted_iota(jnp.int32, (chunk // 8,) + lanes, 0) * 8 + lax.broadcasted_iota(
        jnp.int32, (chunk // 8,) + lanes, 1
    )

    def part(row):
        return logit_buf[row : row + chunk, :].reshape((chunk // 8,) + lanes)

    def reduce(entry):
        k, g = scalars[at_set + entry], scalars[at_group + entry]
        top_before = state[k, 0]
        top = top_before
        for row in range(0, GROUP, chunk):
            top = jnp.maximum(top, jnp.max(part(row), axis=0))
        shift = top_before - top
        scale = jnp.exp(shift)
        total_before = state[k, 1]
        total = total_before * scale
        moment = (state[k, 2] + shift * total_before) * scale
        picked = state[k, 3]
        for half in range(2):
            wanted = wanted_buf[k] - scalars[at_base + 2 * g + half]
            for row in range(0, PIECE, chunk):
                logits = part(half * PIECE + row)
                under = logits - top[None]
                weight = jnp.exp(under)
                total += jnp.sum(weight, axis=0)
                moment += jnp.sum(weight * under, axis=0)
                picked += jnp.sum(jnp.where(rows == (wanted - row)[None], logits, 0.0), axis=0)
        state[k, 0] = top
        state[k, 1] = total
        state[k, 2] = moment
        state[k, 3] = picked

    def body(u, carry):
        for ahead in range(2, n_groups):

            @pl.when(u + 2 == ahead)
            def _():
                fetch(ahead)

        @pl.when(u < n_groups)
        def _():
            for half in range(2):
                pltpu.make_async_copy(
                    head_refs[0].at[pl.ds(0, PIECE)],
                    head_buf.at[pl.ds(u * GROUP + half * PIECE, PIECE)],
                    head_sem.at[2 * u + half],
                ).wait()

        reduce(u)
        k, g = scalars[at_set + u + 1], scalars[at_group + u + 1]
        logit_buf[...] = lax.dot_general(
            head_buf[pl.ds(pl.multiple_of(g * GROUP, GROUP), GROUP), :],
            tok_buf[k],
            (((1,), (1,)), ((), ())),
            preferred_element_type=jnp.float32,
        )
        return carry

    lax.fori_loop(0, n_units, body, 0)
    reduce(n_units)
    for k in range(n_sets):
        top8 = state[k, 0]
        top = jnp.max(top8, axis=0, keepdims=True)
        shift = top8 - top
        scale = jnp.exp(shift)
        to = out_ref.at[z ^ (NZ - 1)] if final else out_ref.at[k]
        to[0:1, :] = top
        to[1:2, :] = jnp.sum(state[k, 1] * scale, axis=0, keepdims=True)
        to[2:3, :] = jnp.sum((state[k, 2] + shift * state[k, 1]) * scale, axis=0, keepdims=True)
        to[3:4, :] = jnp.sum(state[k, 3], axis=0, keepdims=True)
        to[4:5, :] = notes[k]
        to[5:8, :] = jnp.zeros((3, TILE), jnp.float32)
    if final:
        for k in range(n_known):
            out_ref[z ^ k] = known_ref[k]


def statistics(name, z, offset, sets, heads, plan, known=None, final=False):
    arrays, head_plan = [], []
    for array, start, _ in heads:
        for index, seen in enumerate(arrays):
            if seen is array:
                break
        else:
            index = len(arrays)
            arrays.append(array)
        head_plan.append((index, start))
    n_groups = len(heads) // 2
    units = [(k, g) for k, first, last in plan for g in range(first, last)]
    fixed = [units[0][0]] + [k for k, _ in units] + [n_groups] + [g for _, g in units]
    scalars = jnp.concatenate(
        [
            jnp.stack([z, offset]),
            jnp.array(fixed, jnp.int32),
            jnp.stack([base for _, _, base in heads]),
            jnp.array([1 << 30, 1 << 30], jnp.int32),
        ]
    ).astype(jnp.int32)
    width = arrays[0].shape[1]
    vocab = len(heads) * PIECE
    before = [] if known is None else [known]
    n_known = 0 if known is None else known.shape[0]
    n_out = NZ if final else len(sets)
    pairs = len(units) * GROUP * TILE
    return pl.pallas_call(
        functools.partial(stats_kernel, units, len(sets), n_known, final, head_plan),
        grid_spec=pltpu.PrefetchScalarGridSpec(
            num_scalar_prefetch=1,
            grid=(1,),
            in_specs=[pl.BlockSpec(array.shape, lambda i, s: (0, 0, 0)) for array in before]
            + [pl.BlockSpec(memory_space=pl.ANY)] * (2 * len(sets) + len(arrays)),
            out_specs=pl.BlockSpec((n_out, 8, TILE), lambda i, s: (0, 0, 0)),
            scratch_shapes=[
                pltpu.VMEM((len(sets), TILE, width), jnp.bfloat16),
                pltpu.VMEM((vocab, width), jnp.bfloat16),
                pltpu.VMEM((GROUP, TILE), jnp.float32),
                pltpu.VMEM((len(sets), 4, 8, TILE), jnp.float32),
                pltpu.VMEM((len(sets), 1, TILE), jnp.int32),
                pltpu.SemaphoreType.DMA((2 * len(sets),)),
                pltpu.SemaphoreType.DMA((len(heads),)),
            ],
        ),
        out_shape=jax.ShapeDtypeStruct((n_out, 8, TILE), jnp.float32),
        compiler_params=pltpu.CompilerParams(vmem_limit_bytes=58 * 1024 * 1024),
        cost_estimate=pl.CostEstimate(
            flops=2 * pairs * width,
            bytes_accessed=2 * (len(sets) * TILE + vocab) * width,
            transcendentals=pairs,
        ),
        name=name,
    )(scalars, *before, *[half for pair in sets for half in pair], *arrays)


def after(values, *deps):
    return lax.optimization_barrier((values, deps))[0]


def join(parts):
    top = functools.reduce(jnp.maximum, [part[0] for part in parts])
    total = moment = picked = 0.0
    for part in parts:
        shift = part[0] - top
        scale = jnp.exp(shift)
        total += part[1] * scale
        moment += (part[2] + shift * part[1]) * scale
        picked += part[3]
    return top, total, moment, picked


def on_device(hidden, gain, head, targets, lengths, group_map):
    tok = lax.axis_index("tok")
    vocab = lax.axis_index("vocab")
    z, y = tok // NY, tok % NY
    x, core = vocab // 2, vocab % 2
    upper = z >= NZ // 2
    quarter = jnp.where(upper, VOCAB - 1 - vocab, vocab)

    zs = jnp.arange(NZ)

    sure, rest_own, trade = prepare(hidden, gain, targets, quarter)
    traded = across(trade, 2)
    sizes_own = after(jnp.concatenate([lengths, group_map[:, 0]]), sure)
    load = jnp.sum(sizes_own[:8])
    block_start = (jnp.arange(4) * VOCAB + quarter) * SURE
    live = jnp.sum(jnp.clip(load - block_start, 0, SURE))
    level = jnp.arange(NOTES)[:, None]
    sizes_own = jnp.pad(sizes_own, (0, TILE - 16))[None, :]
    sizes_own = jnp.where(level == 2, sizes_own & 127, jnp.where(level == 3, sizes_own >> 7, 0))

    rest = merge(live, rest_own, traded, sizes_own.astype(jnp.float32))
    sure_1, sure_2 = across(sure, 1), across(after(sure, traded), 2)
    rest_1, rest_2 = across(rest, 1), across(rest, 2)
    sure_3 = across(sure_2, 1)

    low_half, high_half = head[:PIECE], head[PIECE:]
    xa, ya = to_x(low_half), to_y(high_half)
    high_later, low_later = after((high_half, low_half), xa, ya)
    xb, yb = to_x(high_later), to_y(low_later)

    def base(at_y, at_x, at_core, half):
        return ((at_y * 2 + at_x) * 2 + at_core) * GROUP + half * PIECE

    def both_cores(piece, at_y, at_x, half):
        return [
            (piece, 0, base(at_y, at_x, core, half)),
            (to_core(piece), 0, base(at_y, at_x, 1 - core, half)),
        ]

    head_core = to_core(head)
    heads_own = [
        (array, half * PIECE, base(y, x, at_core, half))
        for array, at_core in ((head, core), (head_core, 1 - core))
        for half in range(2)
    ]
    xa_later, ya_later = after((xa, ya), traded)
    heads = heads_own + both_cores(xa_later, y, 1 - x, 0) + both_cores(ya_later, 1 - y, x, 1)
    offset = z * (TOK * VOCAB // NZ * head.shape[0])
    run = functools.partial(statistics, z=z, offset=offset)

    x2, y2 = to_x(after(ya, xb, yb)), to_y(after(xa, xb, yb))
    heads = heads + both_cores(xb, y, 1 - x, 1) + both_cores(yb, 1 - y, x, 0)
    early = run(
        "first",
        sets=[(sure, rest), (sure_1, rest_1)],
        heads=heads,
        plan=[(0, 0, 6), (1, 0, 6)],
    )
    rest_2, sure_3, x2, y2 = after((rest_2, sure_3, x2, y2), early)
    rest_3 = across(rest_2, 1)
    heads = heads + both_cores(x2, 1 - y, 1 - x, 1) + both_cores(y2, 1 - y, 1 - x, 0)
    early = run(
        "second",
        sets=[(sure, rest), (sure_1, rest_1), (sure_2, rest_2)],
        heads=heads,
        plan=[(2, 0, 8), (0, 6, 8), (1, 6, 8)],
        known=early,
    )
    rest_3 = after(rest_3, early)
    own_stats = run(
        "third", sets=[(sure_3, rest_3)], heads=heads, plan=[(0, 0, 8)], known=early, final=True
    )

    parts = [own_stats] + [across(own_stats, step) for step in (1, 2, 3)]
    top, total, moment, picked = join([jnp.moveaxis(part[:, :4, :EVEN], 1, 0) for part in parts])
    spread = jnp.log(total)
    logprob = picked - top - spread
    entropy = spread - moment / total
    partner = jnp.array([2, 3, 0, 1])
    sizes = own_stats[:, 4, :16].astype(jnp.int32)
    own_lengths = sizes[:, :8]
    loads = jnp.sum(own_lengths, axis=1)
    quarters = jnp.where(zs >= NZ // 2, VOCAB - 1 - vocab, vocab)
    starts_of = (jnp.arange(4)[None, :] * VOCAB + quarters[:, None]) * SURE
    lives = jnp.sum(jnp.clip(loads[:, None] - starts_of, 0, SURE), axis=1)
    slots = jnp.arange(EVEN)
    stays = slots[None, :] < lives[:, None]

    local = jnp.where(stays, slots[None, :], 2 * EVEN - 1 - slots[None, :])
    origin = jnp.where(stays, zs[:, None], partner[:, None])
    origin_quarter = jnp.where(origin >= NZ // 2, VOCAB - 1 - vocab, vocab)
    row = (local // SURE * VOCAB + origin_quarter) * SURE + local % SURE
    place = origin * hidden.shape[0] + row
    finish = jnp.cumsum(own_lengths, axis=1) + zs[:, None] * hidden.shape[0]
    begin = finish - own_lengths
    member = (place[:, :, None, None] >= begin) & (place[:, :, None, None] < finish)
    sums_part = jnp.sum(jnp.where(member, logprob[:, :, None, None], 0.0), axis=(0, 1))

    results = jnp.stack([logprob, entropy])
    mine = lax.dynamic_index_in_dim(results, z, 1, False)
    theirs = lax.dynamic_index_in_dim(results, z ^ 2, 1, False)
    local_rows = jnp.concatenate([mine, jnp.flip(theirs[:, SURE:], 1)], 1)
    local_rows = jnp.where(jnp.arange(SHARE)[None, :] < live, local_rows, 0.0)
    gathered = lax.all_gather(
        jnp.concatenate([local_rows.reshape(1, -1), sums_part.reshape(1, -1)], 1), "vocab"
    ).reshape(VOCAB, -1)
    sums_own = jnp.concatenate(
        [
            jnp.sum(gathered[:, 2 * SHARE :], axis=0).reshape(NZ, 8),
            sizes.astype(jnp.float32),
        ],
        1,
    )
    sums_other = to_y(sums_own)
    sums = jnp.where(
        y == 0, jnp.stack([sums_own, sums_other], 1), jnp.stack([sums_other, sums_own], 1)
    )
    all_lengths, all_groups = sums[:, :, 8:16], sums[:, :, 16:].astype(jnp.int32)
    sums = sums[:, :, :8]
    parts = gathered[:, : 2 * SHARE].reshape(VOCAB, 2, SHARE)
    parts = lax.dynamic_slice_in_dim(parts, vocab * SURE, SURE, 2)
    parts = jnp.where(upper, jnp.flip(parts, 0), parts)
    out = parts.transpose(1, 0, 2).reshape(2, SHARE)

    means = (sums / all_lengths).reshape(-1)
    onehot = (
        all_groups.reshape(-1)[:, None] == jnp.arange(TOK, dtype=jnp.int32)[None, :]
    ).astype(jnp.float32)
    group_mean = jnp.sum(onehot * means[:, None], axis=0) / jnp.sum(onehot, axis=0)
    centered = means - jnp.sum(onehot * group_mean[None, :], axis=1)
    return out[0], out[1], lax.dynamic_slice_in_dim(centered, tok * 8 + vocab * 2, 2, 0)


def solution(mesh):
    fits = mesh.shape["tok"] == TOK and mesh.shape["vocab"] == VOCAB
    return jax.shard_map(
        on_device if fits else on_any_mesh,
        mesh=mesh,
        in_specs=(
            P("tok", None),
            P(),
            P(("tok", "vocab"), None),
            P("tok"),
            P("tok"),
            P("tok", None),
        ),
        out_specs=(P(("tok", "vocab")), P(("tok", "vocab")), P(("tok", "vocab"))),
        check_vma=False,
    )
```

```python
import functools

import jax
import jax.numpy as jnp
from jax import lax
from jax.experimental import pallas as pl
from jax.experimental.pallas import tpu as pltpu
from jax.sharding import PartitionSpec as P

EPS = 1e-06
LOW = -1e30
BOTH = ("tok", "vocab")
TOK, VOCAB, NZ, NY = 8, 4, 4, 2


def combined_all(value, axis, join):
    pieces = jax.tree.map(lambda part: lax.all_gather(part, axis), value)
    head = jax.tree.map(lambda part: part[0], pieces)
    tail = jax.tree.map(lambda part: part[1:], pieces)
    so_far, _ = lax.scan(lambda so_far, piece: (join(so_far, piece), None), head, tail)
    return so_far


def normalize(states, gain):
    values = states.astype(jnp.float32)
    scale_inv = lax.rsqrt(jnp.mean(values * values, axis=-1, keepdims=True) + EPS)
    return (values * scale_inv * gain).astype(jnp.bfloat16)


def combine(left_part, right_part):
    highest = jnp.maximum(left_part[0], right_part[0])
    left_scale = jnp.exp(left_part[0] - highest)
    right_scale = jnp.exp(right_part[0] - highest)
    return (
        highest,
        left_part[1] * left_scale + right_part[1] * right_scale,
        left_part[2] * left_scale + right_part[2] * right_scale,
        left_part[3] + right_part[3],
    )


def score(states, wanted, gain, head):
    normed = normalize(states, gain[None, :])
    logits = jnp.einsum(
        "nd,vd->nv",
        normed,
        lax.all_gather(head, "tok", axis=0, tiled=True),
        preferred_element_type=jnp.float32,
    )
    vocab_block = head.shape[0]
    vocab_shards = lax.axis_size("vocab")
    shard_index = lax.axis_index("vocab")
    owned = wanted // vocab_block % vocab_shards == shard_index
    column = wanted // (vocab_block * vocab_shards) * vocab_block + wanted % vocab_block
    column = jnp.where(owned, column, -1)
    columns = lax.broadcasted_iota(jnp.int32, logits.shape, 1)
    highest = jnp.max(logits, axis=1)
    exponent = jnp.exp(logits - highest[:, None])
    exp_total = jnp.sum(exponent, axis=1)
    moment = jnp.sum(exponent * logits, axis=1)
    picked = jnp.sum(jnp.where(columns == column[:, None], logits, 0.0), axis=1)
    highest, exp_total, moment, picked = combined_all(
        (highest, exp_total, moment, picked), "vocab", combine
    )
    log_total = highest + jnp.log(exp_total)
    return (picked - log_total, log_total - moment / exp_total)


def on_any_mesh(hidden, gain, head, targets, lengths, group_map):
    capacity = hidden.shape[0]
    own_load = jnp.sum(lengths)
    slot_index = jnp.arange(capacity, dtype=jnp.int32)
    logprob, entropy = score(hidden, targets, gain, head)
    is_live = slot_index < own_load
    logprob = jnp.where(is_live, logprob, 0.0)
    entropy = jnp.where(is_live, entropy, 0.0)
    finish = jnp.cumsum(lengths)
    starts = finish - lengths
    member = (
        (slot_index[:, None] >= starts[None, :]) & (slot_index[:, None] < finish[None, :])
    ).astype(jnp.float32)
    request_sums = jnp.sum(member * logprob[:, None], axis=0)
    mean_logprob = request_sums / lengths.astype(jnp.float32)
    groups_count = lengths.shape[0] * lax.axis_size("tok") // 8
    onehot = (
        group_map[:, 0][:, None] == jnp.arange(groups_count, dtype=jnp.int32)[None, :]
    ).astype(jnp.float32)
    group_sums, counts = lax.psum(
        (jnp.sum(onehot * mean_logprob[:, None], axis=0), jnp.sum(onehot, axis=0)), "tok"
    )
    group_mean = group_sums / counts
    centered = mean_logprob - jnp.sum(onehot * group_mean[None, :], axis=1)
    vocab_shards = lax.axis_size("vocab")
    shard_index = lax.axis_index("vocab")
    slot_share = capacity // vocab_shards
    request_share = lengths.shape[0] // vocab_shards
    return (
        lax.dynamic_slice_in_dim(logprob, shard_index * slot_share, slot_share, 0),
        lax.dynamic_slice_in_dim(entropy, shard_index * slot_share, slot_share, 0),
        lax.dynamic_slice_in_dim(centered, shard_index * request_share, request_share, 0),
    )


def device_pairs(target):
    pairs = []
    for z in range(NZ):
        for y in range(NY):
            for x in range(2):
                for c in range(2):
                    to = target(z, y, x, c)
                    if to is not None:
                        pairs.append(
                            ((z * NY + y) * VOCAB + x * 2 + c, (to[0] * NY + to[1]) * VOCAB + to[2] * 2 + to[3])
                        )
    return pairs


def send(value, target):
    return lax.ppermute(value, BOTH, device_pairs(target))


def to_x(value):
    return send(value, lambda z, y, x, c: (z, y, 1 - x, c))


def to_y(value):
    return send(value, lambda z, y, x, c: (z, 1 - y, x, c))


def to_core(value):
    return send(value, lambda z, y, x, c: (z, y, x, 1 - c))


def across(value, step):
    return send(value, lambda z, y, x, c: (z ^ step, y, x, c))


SHARE = 384
EVEN = 240
SURE = 96
REST = EVEN - SURE
TILE = 256
NOTES = TILE - EVEN
PIECE = 256
GROUP = 2 * PIECE


def prep_kernel(which, h0, h1, h2, h3, gain_ref, tgt_ref, sure_ref, own_ref, trade_ref):
    gain = gain_ref[...]
    slots_count = tgt_ref.shape[1]
    row = lax.broadcasted_iota(jnp.int32, (SURE, SURE), 0)
    col = lax.broadcasted_iota(jnp.int32, (SURE, SURE), 1)
    mirror = (row + col == SURE - 1).astype(jnp.bfloat16)

    def flip(block):
        return jnp.dot(mirror, block, preferred_element_type=jnp.float32).astype(jnp.bfloat16)

    sure_ref[...] = normalize(h0[...], gain)
    own_ref[0:SURE, :] = normalize(h1[...], gain)
    third = normalize(h2[...], gain)
    own_ref[SURE:REST, :] = third[0 : REST - SURE, :]
    trade_ref[0:SURE, :] = flip(normalize(h3[...], gain))
    trade_ref[SURE:REST, :] = flip(third)[0 : REST - SURE, :]

    wanted = tgt_ref[...]
    level = lax.broadcasted_iota(jnp.int32, (NOTES, slots_count), 0)
    digits = jnp.where(level == 0, wanted & 127, jnp.where(level == 1, wanted >> 7, 0))
    digits = digits.astype(jnp.float32).astype(jnp.bfloat16)
    source = lax.broadcasted_iota(jnp.int32, (slots_count, TILE), 0)
    lane = lax.broadcasted_iota(jnp.int32, (1, TILE), 1)

    def notes(local, keep):
        block = (
            (local >= SURE).astype(jnp.int32)
            + (local >= 2 * SURE).astype(jnp.int32)
            + (local >= 3 * SURE).astype(jnp.int32)
        )
        at = local + block * ((VOCAB - 1) * SURE) + which[0] * SURE
        at = jnp.where(keep, at, -1)
        pick = jnp.where(source == at, 1.0, 0.0).astype(jnp.bfloat16)
        return jnp.dot(digits, pick, preferred_element_type=jnp.float32).astype(jnp.bfloat16)

    own_ref[REST : REST + NOTES, :] = jnp.zeros((NOTES, own_ref.shape[1]), jnp.bfloat16)
    own_ref[REST : REST + NOTES, 0:TILE] = notes(lane, lane < EVEN)
    trade_ref[REST : REST + NOTES, :] = jnp.zeros((NOTES, own_ref.shape[1]), jnp.bfloat16)
    trade_ref[REST : REST + NOTES, 0:TILE] = notes(
        2 * EVEN - 1 - lane, (lane >= SURE) & (lane < EVEN)
    )


def prepare(hidden, gain, targets, quarter):
    width = hidden.shape[1]

    def block(j):
        return pl.BlockSpec((SURE, width), lambda i, which, j=j: (VOCAB * j + which[0], 0))

    def whole(*shape):
        return pl.BlockSpec(shape, lambda i, which: (0, 0))

    return pl.pallas_call(
        prep_kernel,
        grid_spec=pltpu.PrefetchScalarGridSpec(
            num_scalar_prefetch=1,
            grid=(1,),
            in_specs=[block(j) for j in range(4)] + [whole(1, width), whole(1, targets.shape[0])],
            out_specs=[whole(n, width) for n in (SURE, REST + NOTES, REST + NOTES)],
        ),
        out_shape=[
            jax.ShapeDtypeStruct((n, width), jnp.bfloat16) for n in (SURE, REST + NOTES, REST + NOTES)
        ],
        cost_estimate=pl.CostEstimate(flops=4 * 10**8, bytes_accessed=3 * 10**6, transcendentals=SHARE),
        name="prep",
    )(quarter.reshape(1), hidden, hidden, hidden, hidden, gain[None, :], targets[None, :])


def merge_kernel(live_ref, own_ref, traded_ref, sizes_ref, out_ref):
    live = live_ref[0]
    for low in range(0, REST, 48):
        slot = lax.broadcasted_iota(jnp.int32, (48, own_ref.shape[1]), 0) + (SURE + low)
        out_ref[low : low + 48, :] = jnp.where(
            slot < live,
            own_ref[low : low + 48, :].astype(jnp.float32),
            traded_ref[low : low + 48, :].astype(jnp.float32),
        ).astype(jnp.bfloat16)
    lane = lax.broadcasted_iota(jnp.int32, (NOTES, TILE), 1)
    out_ref[REST : REST + NOTES, :] = jnp.zeros((NOTES, own_ref.shape[1]), jnp.bfloat16)
    out_ref[REST : REST + NOTES, 0:TILE] = (
        jnp.where(
            lane < live,
            own_ref[REST : REST + NOTES, 0:TILE].astype(jnp.float32),
            traded_ref[REST : REST + NOTES, 0:TILE].astype(jnp.float32),
        )
        + sizes_ref[...]
    ).astype(jnp.bfloat16)


def merge(live, own, traded, sizes):
    def whole(array):
        return pl.BlockSpec(array.shape, lambda i, s: (0, 0))

    return pl.pallas_call(
        merge_kernel,
        grid_spec=pltpu.PrefetchScalarGridSpec(
            num_scalar_prefetch=1,
            grid=(1,),
            in_specs=[whole(own), whole(traded), whole(sizes)],
            out_specs=whole(own),
        ),
        out_shape=jax.ShapeDtypeStruct(own.shape, own.dtype),
        cost_estimate=pl.CostEstimate(flops=10**6, bytes_accessed=3 * 10**6, transcendentals=0),
        name="merge",
    )(live.reshape(1), own, traded, sizes)


def stats_kernel(units, n_sets, n_known, final, head_plan, scalars, *refs):
    known_ref = refs[0] if n_known else None
    refs = refs[1:] if n_known else refs
    tok_refs = refs[: 2 * n_sets]
    n_head_refs = 1 + max(index for index, _ in head_plan)
    head_refs = refs[2 * n_sets : 2 * n_sets + n_head_refs]
    (out_ref, tok_buf, head_buf, logit_buf, state, wanted_buf, tok_sem, head_sem) = refs[
        2 * n_sets + n_head_refs :
    ]
    n_groups = len(head_plan) // 2
    n_units = len(units)
    at_set, at_group, at_base = 2, 2 + n_units + 1, 2 + 2 * (n_units + 1)
    z, offset = scalars[0], scalars[1]
    lanes = (8, TILE)

    def fetch(g):
        for piece in (2 * g, 2 * g + 1):
            index, start = head_plan[piece]
            pltpu.make_async_copy(
                head_refs[index].at[pl.ds(start, PIECE)],
                head_buf.at[pl.ds(piece * PIECE, PIECE)],
                head_sem.at[piece],
            ).start()

    def tok_copy(half):
        return pltpu.make_async_copy(
            tok_refs[half],
            tok_buf.at[half // 2, pl.ds(SURE * (half % 2), tok_refs[half].shape[0])],
            tok_sem.at[half],
        )

    for half in range(2 * n_sets):
        tok_copy(half).start()
    for g in range(min(2, n_groups)):
        fetch(g)
    logit_buf[...] = jnp.full(logit_buf.shape, LOW, jnp.float32)
    for k in range(n_sets):
        state[k, 0] = jnp.full(lanes, LOW, jnp.float32)
        for row in range(1, 4):
            state[k, row] = jnp.zeros(lanes, jnp.float32)
    if not final:
        for k in range(n_known):
            for row in range(4):
                state[k, row, 0:1, :] = known_ref[k, row : row + 1, :]
    notes = []
    for k in range(n_sets):
        tok_copy(2 * k).wait()
        tok_copy(2 * k + 1).wait()
        digits = tok_buf[k, EVEN:TILE, 0:TILE].astype(jnp.float32)
        wanted_buf[k] = (digits[0:1, :] + 128.0 * digits[1:2, :]).astype(jnp.int32) - offset
        notes.append(digits[2:3, :] + 128.0 * digits[3:4, :])
    chunk = 64
    rows = lax.broadcasted_iota(jnp.int32, (chunk // 8,) + lanes, 0) * 8 + lax.broadcasted_iota(
        jnp.int32, (chunk // 8,) + lanes, 1
    )

    def part(row):
        return logit_buf[row : row + chunk, :].reshape((chunk // 8,) + lanes)

    def reduce(entry):
        k, g = scalars[at_set + entry], scalars[at_group + entry]
        top_before = state[k, 0]
        top = top_before
        for row in range(0, GROUP, chunk):
            top = jnp.maximum(top, jnp.max(part(row), axis=0))
        shift = top_before - top
        scale = jnp.exp(shift)
        total_before = state[k, 1]
        total = total_before * scale
        moment = (state[k, 2] + shift * total_before) * scale
        picked = state[k, 3]
        for half in range(2):
            wanted = wanted_buf[k] - scalars[at_base + 2 * g + half]
            for row in range(0, PIECE, chunk):
                logits = part(half * PIECE + row)
                under = logits - top[None]
                weight = jnp.exp(under)
                total += jnp.sum(weight, axis=0)
                moment += jnp.sum(weight * under, axis=0)
                picked += jnp.sum(jnp.where(rows == (wanted - row)[None], logits, 0.0), axis=0)
        state[k, 0] = top
        state[k, 1] = total
        state[k, 2] = moment
        state[k, 3] = picked

    def body(u, carry):
        for ahead in range(2, n_groups):

            @pl.when(u + 2 == ahead)
            def _():
                fetch(ahead)

        @pl.when(u < n_groups)
        def _():
            for half in range(2):
                pltpu.make_async_copy(
                    head_refs[0].at[pl.ds(0, PIECE)],
                    head_buf.at[pl.ds(u * GROUP + half * PIECE, PIECE)],
                    head_sem.at[2 * u + half],
                ).wait()

        reduce(u)
        k, g = scalars[at_set + u + 1], scalars[at_group + u + 1]
        logit_buf[...] = lax.dot_general(
            head_buf[pl.ds(pl.multiple_of(g * GROUP, GROUP), GROUP), :],
            tok_buf[k],
            (((1,), (1,)), ((), ())),
            preferred_element_type=jnp.float32,
        )
        return carry

    lax.fori_loop(0, n_units, body, 0)
    reduce(n_units)
    for k in range(n_sets):
        top8 = state[k, 0]
        top = jnp.max(top8, axis=0, keepdims=True)
        shift = top8 - top
        scale = jnp.exp(shift)
        to = out_ref.at[z ^ (NZ - 1)] if final else out_ref.at[k]
        to[0:1, :] = top
        to[1:2, :] = jnp.sum(state[k, 1] * scale, axis=0, keepdims=True)
        to[2:3, :] = jnp.sum((state[k, 2] + shift * state[k, 1]) * scale, axis=0, keepdims=True)
        to[3:4, :] = jnp.sum(state[k, 3], axis=0, keepdims=True)
        to[4:5, :] = notes[k]
        to[5:8, :] = jnp.zeros((3, TILE), jnp.float32)
    if final:
        for k in range(n_known):
            out_ref[z ^ k] = known_ref[k]


def statistics(name, z, offset, sets, heads, plan, known=None, final=False):
    arrays, head_plan = [], []
    for array, start, _ in heads:
        for index, seen in enumerate(arrays):
            if seen is array:
                break
        else:
            index = len(arrays)
            arrays.append(array)
        head_plan.append((index, start))
    n_groups = len(heads) // 2
    units = [(k, g) for k, first, last in plan for g in range(first, last)]
    fixed = [units[0][0]] + [k for k, _ in units] + [n_groups] + [g for _, g in units]
    scalars = jnp.concatenate(
        [
            jnp.stack([z, offset]),
            jnp.array(fixed, jnp.int32),
            jnp.stack([base for _, _, base in heads]),
            jnp.array([1 << 30, 1 << 30], jnp.int32),
        ]
    ).astype(jnp.int32)
    width = arrays[0].shape[1]
    vocab = len(heads) * PIECE
    before = [] if known is None else [known]
    n_known = 0 if known is None else known.shape[0]
    n_out = NZ if final else len(sets)
    pairs = len(units) * GROUP * TILE
    return pl.pallas_call(
        functools.partial(stats_kernel, units, len(sets), n_known, final, head_plan),
        grid_spec=pltpu.PrefetchScalarGridSpec(
            num_scalar_prefetch=1,
            grid=(1,),
            in_specs=[pl.BlockSpec(array.shape, lambda i, s: (0, 0, 0)) for array in before]
            + [pl.BlockSpec(memory_space=pl.ANY)] * (2 * len(sets) + len(arrays)),
            out_specs=pl.BlockSpec((n_out, 8, TILE), lambda i, s: (0, 0, 0)),
            scratch_shapes=[
                pltpu.VMEM((len(sets), TILE, width), jnp.bfloat16),
                pltpu.VMEM((vocab, width), jnp.bfloat16),
                pltpu.VMEM((GROUP, TILE), jnp.float32),
                pltpu.VMEM((len(sets), 4, 8, TILE), jnp.float32),
                pltpu.VMEM((len(sets), 1, TILE), jnp.int32),
                pltpu.SemaphoreType.DMA((2 * len(sets),)),
                pltpu.SemaphoreType.DMA((len(heads),)),
            ],
        ),
        out_shape=jax.ShapeDtypeStruct((n_out, 8, TILE), jnp.float32),
        compiler_params=pltpu.CompilerParams(vmem_limit_bytes=61 * 1024 * 1024),
        cost_estimate=pl.CostEstimate(
            flops=2 * pairs * width,
            bytes_accessed=2 * (len(sets) * TILE + vocab) * width,
            transcendentals=pairs,
        ),
        name=name,
    )(scalars, *before, *[half for pair in sets for half in pair], *arrays)


def after(values, *deps):
    return lax.optimization_barrier((values, deps))[0]


def join(parts):
    top = functools.reduce(jnp.maximum, [part[0] for part in parts])
    total = moment = picked = 0.0
    for part in parts:
        shift = part[0] - top
        scale = jnp.exp(shift)
        total += part[1] * scale
        moment += (part[2] + shift * part[1]) * scale
        picked += part[3]
    return top, total, moment, picked


def on_device(hidden, gain, head, targets, lengths, group_map):
    tok = lax.axis_index("tok")
    vocab = lax.axis_index("vocab")
    z, y = tok // NY, tok % NY
    x, core = vocab // 2, vocab % 2
    upper = z >= NZ // 2
    quarter = jnp.where(upper, VOCAB - 1 - vocab, vocab)

    zs = jnp.arange(NZ)

    sure, rest_own, trade = prepare(hidden, gain, targets, quarter)
    traded = across(trade, 2)
    sizes_own = after(jnp.concatenate([lengths, group_map[:, 0]]), sure)
    load = jnp.sum(sizes_own[:8])
    block_start = (jnp.arange(4) * VOCAB + quarter) * SURE
    live = jnp.sum(jnp.clip(load - block_start, 0, SURE))
    level = jnp.arange(NOTES)[:, None]
    sizes_own = jnp.pad(sizes_own, (0, TILE - 16))[None, :]
    sizes_own = jnp.where(level == 2, sizes_own & 127, jnp.where(level == 3, sizes_own >> 7, 0))

    rest = merge(live, rest_own, traded, sizes_own.astype(jnp.float32))
    sure_1, sure_2 = across(sure, 1), across(after(sure, traded), 2)
    rest_1, rest_2 = across(rest, 1), across(rest, 2)
    sure_3 = across(sure_2, 1)

    head_later = after(head, sure)
    low_half, high_half = head_later[:PIECE], head_later[PIECE:]
    xa, ya = to_x(low_half), to_y(high_half)
    high_later, low_later = after((high_half, low_half), xa, ya)
    xb, yb = to_x(high_later), to_y(low_later)

    def base(at_y, at_x, at_core, half):
        return ((at_y * 2 + at_x) * 2 + at_core) * GROUP + half * PIECE

    def both_cores(piece, at_y, at_x, half):
        return [
            (piece, 0, base(at_y, at_x, core, half)),
            (to_core(piece), 0, base(at_y, at_x, 1 - core, half)),
        ]

    head_core = to_core(head)
    heads_own = [
        (array, half * PIECE, base(y, x, at_core, half))
        for array, at_core in ((head, core), (head_core, 1 - core))
        for half in range(2)
    ]
    xa_later, ya_later = after((xa, ya), traded)
    heads = heads_own + both_cores(xa_later, y, 1 - x, 0) + both_cores(ya_later, 1 - y, x, 1)
    offset = z * (TOK * VOCAB // NZ * head.shape[0])
    run = functools.partial(statistics, z=z, offset=offset)

    x2, y2 = to_x(after(ya, xb, yb)), to_y(after(xa, xb, yb))
    heads = heads + both_cores(xb, y, 1 - x, 1) + both_cores(yb, 1 - y, x, 0)
    early = run(
        "first",
        sets=[(sure, rest), (sure_1, rest_1)],
        heads=heads,
        plan=[(0, 0, 6), (1, 0, 6)],
    )
    rest_2, sure_3, x2, y2 = after((rest_2, sure_3, x2, y2), early)
    rest_3 = across(rest_2, 1)
    heads = heads + both_cores(x2, 1 - y, 1 - x, 1) + both_cores(y2, 1 - y, 1 - x, 0)
    early = run(
        "second",
        sets=[(sure, rest), (sure_1, rest_1), (sure_2, rest_2)],
        heads=heads,
        plan=[(2, 0, 8), (0, 6, 8), (1, 6, 8)],
        known=early,
    )
    rest_3 = after(rest_3, early)
    own_stats = run(
        "third", sets=[(sure_3, rest_3)], heads=heads, plan=[(0, 0, 8)], known=early, final=True
    )

    parts = [own_stats] + [across(own_stats, step) for step in (1, 2, 3)]
    top, total, moment, picked = join([jnp.moveaxis(part[:, :4, :EVEN], 1, 0) for part in parts])
    spread = jnp.log(total)
    logprob = picked - top - spread
    entropy = spread - moment / total
    partner = jnp.array([2, 3, 0, 1])
    sizes = own_stats[:, 4, :16].astype(jnp.int32)
    own_lengths = sizes[:, :8]
    loads = jnp.sum(own_lengths, axis=1)
    quarters = jnp.where(zs >= NZ // 2, VOCAB - 1 - vocab, vocab)
    starts_of = (jnp.arange(4)[None, :] * VOCAB + quarters[:, None]) * SURE
    lives = jnp.sum(jnp.clip(loads[:, None] - starts_of, 0, SURE), axis=1)
    slots = jnp.arange(EVEN)
    stays = slots[None, :] < lives[:, None]

    local = jnp.where(stays, slots[None, :], 2 * EVEN - 1 - slots[None, :])
    origin = jnp.where(stays, zs[:, None], partner[:, None])
    origin_quarter = jnp.where(origin >= NZ // 2, VOCAB - 1 - vocab, vocab)
    row = (local // SURE * VOCAB + origin_quarter) * SURE + local % SURE
    place = origin * hidden.shape[0] + row
    finish = jnp.cumsum(own_lengths, axis=1) + zs[:, None] * hidden.shape[0]
    begin = finish - own_lengths
    member = (place[:, :, None, None] >= begin) & (place[:, :, None, None] < finish)
    sums_part = jnp.sum(jnp.where(member, logprob[:, :, None, None], 0.0), axis=(0, 1))

    results = jnp.stack([logprob, entropy])
    mine = lax.dynamic_index_in_dim(results, z, 1, False)
    theirs = lax.dynamic_index_in_dim(results, z ^ 2, 1, False)
    local_rows = jnp.concatenate([mine, jnp.flip(theirs[:, SURE:], 1)], 1)
    local_rows = jnp.where(jnp.arange(SHARE)[None, :] < live, local_rows, 0.0)
    gathered = lax.all_gather(
        jnp.concatenate([local_rows.reshape(1, -1), sums_part.reshape(1, -1)], 1), "vocab"
    ).reshape(VOCAB, -1)
    sums_own = jnp.concatenate(
        [
            jnp.sum(gathered[:, 2 * SHARE :], axis=0).reshape(NZ, 8),
            sizes.astype(jnp.float32),
        ],
        1,
    )
    sums_other = to_y(sums_own)
    sums = jnp.where(
        y == 0, jnp.stack([sums_own, sums_other], 1), jnp.stack([sums_other, sums_own], 1)
    )
    all_lengths, all_groups = sums[:, :, 8:16], sums[:, :, 16:].astype(jnp.int32)
    sums = sums[:, :, :8]
    parts = gathered[:, : 2 * SHARE].reshape(VOCAB, 2, SHARE)
    parts = lax.dynamic_slice_in_dim(parts, vocab * SURE, SURE, 2)
    parts = jnp.where(upper, jnp.flip(parts, 0), parts)
    out = parts.transpose(1, 0, 2).reshape(2, SHARE)

    means = (sums / all_lengths).reshape(-1)
    onehot = (
        all_groups.reshape(-1)[:, None] == jnp.arange(TOK, dtype=jnp.int32)[None, :]
    ).astype(jnp.float32)
    group_mean = jnp.sum(onehot * means[:, None], axis=0) / jnp.sum(onehot, axis=0)
    centered = means - jnp.sum(onehot * group_mean[None, :], axis=1)
    return out[0], out[1], lax.dynamic_slice_in_dim(centered, tok * 8 + vocab * 2, 2, 0)


def solution(mesh):
    fits = mesh.shape["tok"] == TOK and mesh.shape["vocab"] == VOCAB
    return jax.shard_map(
        on_device if fits else on_any_mesh,
        mesh=mesh,
        in_specs=(
            P("tok", None),
            P(),
            P(("tok", "vocab"), None),
            P("tok"),
            P("tok"),
            P("tok", None),
        ),
        out_specs=(P(("tok", "vocab")), P(("tok", "vocab")), P(("tok", "vocab"))),
        check_vma=False,
    )
```

```python
import functools

import jax
import jax.numpy as jnp
from jax import lax
from jax.experimental import pallas as pl
from jax.experimental.pallas import tpu as pltpu
from jax.sharding import PartitionSpec as P

EPS = 1e-06
LOW = -1e30
BOTH = ("tok", "vocab")
TOK, VOCAB, NZ, NY = 8, 4, 4, 2


def combined_all(value, axis, join):
    pieces = jax.tree.map(lambda part: lax.all_gather(part, axis), value)
    head = jax.tree.map(lambda part: part[0], pieces)
    tail = jax.tree.map(lambda part: part[1:], pieces)
    so_far, _ = lax.scan(lambda so_far, piece: (join(so_far, piece), None), head, tail)
    return so_far


def normalize(states, gain):
    values = states.astype(jnp.float32)
    scale_inv = lax.rsqrt(jnp.mean(values * values, axis=-1, keepdims=True) + EPS)
    return (values * scale_inv * gain).astype(jnp.bfloat16)


def combine(left_part, right_part):
    highest = jnp.maximum(left_part[0], right_part[0])
    left_scale = jnp.exp(left_part[0] - highest)
    right_scale = jnp.exp(right_part[0] - highest)
    return (
        highest,
        left_part[1] * left_scale + right_part[1] * right_scale,
        left_part[2] * left_scale + right_part[2] * right_scale,
        left_part[3] + right_part[3],
    )


def score(states, wanted, gain, head):
    normed = normalize(states, gain[None, :])
    logits = jnp.einsum(
        "nd,vd->nv",
        normed,
        lax.all_gather(head, "tok", axis=0, tiled=True),
        preferred_element_type=jnp.float32,
    )
    vocab_block = head.shape[0]
    vocab_shards = lax.axis_size("vocab")
    shard_index = lax.axis_index("vocab")
    owned = wanted // vocab_block % vocab_shards == shard_index
    column = wanted // (vocab_block * vocab_shards) * vocab_block + wanted % vocab_block
    column = jnp.where(owned, column, -1)
    columns = lax.broadcasted_iota(jnp.int32, logits.shape, 1)
    highest = jnp.max(logits, axis=1)
    exponent = jnp.exp(logits - highest[:, None])
    exp_total = jnp.sum(exponent, axis=1)
    moment = jnp.sum(exponent * logits, axis=1)
    picked = jnp.sum(jnp.where(columns == column[:, None], logits, 0.0), axis=1)
    highest, exp_total, moment, picked = combined_all(
        (highest, exp_total, moment, picked), "vocab", combine
    )
    log_total = highest + jnp.log(exp_total)
    return (picked - log_total, log_total - moment / exp_total)


def on_any_mesh(hidden, gain, head, targets, lengths, group_map):
    capacity = hidden.shape[0]
    own_load = jnp.sum(lengths)
    slot_index = jnp.arange(capacity, dtype=jnp.int32)
    logprob, entropy = score(hidden, targets, gain, head)
    is_live = slot_index < own_load
    logprob = jnp.where(is_live, logprob, 0.0)
    entropy = jnp.where(is_live, entropy, 0.0)
    finish = jnp.cumsum(lengths)
    starts = finish - lengths
    member = (
        (slot_index[:, None] >= starts[None, :]) & (slot_index[:, None] < finish[None, :])
    ).astype(jnp.float32)
    request_sums = jnp.sum(member * logprob[:, None], axis=0)
    mean_logprob = request_sums / lengths.astype(jnp.float32)
    groups_count = lengths.shape[0] * lax.axis_size("tok") // 8
    onehot = (
        group_map[:, 0][:, None] == jnp.arange(groups_count, dtype=jnp.int32)[None, :]
    ).astype(jnp.float32)
    group_sums, counts = lax.psum(
        (jnp.sum(onehot * mean_logprob[:, None], axis=0), jnp.sum(onehot, axis=0)), "tok"
    )
    group_mean = group_sums / counts
    centered = mean_logprob - jnp.sum(onehot * group_mean[None, :], axis=1)
    vocab_shards = lax.axis_size("vocab")
    shard_index = lax.axis_index("vocab")
    slot_share = capacity // vocab_shards
    request_share = lengths.shape[0] // vocab_shards
    return (
        lax.dynamic_slice_in_dim(logprob, shard_index * slot_share, slot_share, 0),
        lax.dynamic_slice_in_dim(entropy, shard_index * slot_share, slot_share, 0),
        lax.dynamic_slice_in_dim(centered, shard_index * request_share, request_share, 0),
    )


def device_pairs(target):
    pairs = []
    for z in range(NZ):
        for y in range(NY):
            for x in range(2):
                for c in range(2):
                    to = target(z, y, x, c)
                    if to is not None:
                        pairs.append(
                            ((z * NY + y) * VOCAB + x * 2 + c, (to[0] * NY + to[1]) * VOCAB + to[2] * 2 + to[3])
                        )
    return pairs


def send(value, target):
    return lax.ppermute(value, BOTH, device_pairs(target))


def to_x(value):
    return send(value, lambda z, y, x, c: (z, y, 1 - x, c))


def to_y(value):
    return send(value, lambda z, y, x, c: (z, 1 - y, x, c))


def to_core(value):
    return send(value, lambda z, y, x, c: (z, y, x, 1 - c))


def across(value, step):
    return send(value, lambda z, y, x, c: (z ^ step, y, x, c))


SHARE = 384
EVEN = 240
SURE = 96
REST = EVEN - SURE
TILE = 256
NOTES = TILE - EVEN
PIECE = 256
GROUP = 2 * PIECE


def prep_kernel(which, h0, h1, h2, h3, gain_ref, tgt_ref, sure_ref, own_ref, trade_ref):
    gain = gain_ref[...]
    tgt_rows, tgt_lanes = tgt_ref.shape
    row = lax.broadcasted_iota(jnp.int32, (SURE, SURE), 0)
    col = lax.broadcasted_iota(jnp.int32, (SURE, SURE), 1)
    mirror = (row + col == SURE - 1).astype(jnp.bfloat16)

    def flip(block):
        return jnp.dot(mirror, block, preferred_element_type=jnp.float32).astype(jnp.bfloat16)

    sure_ref[...] = normalize(h0[...], gain)
    own_ref[0:SURE, :] = normalize(h1[...], gain)
    third = normalize(h2[...], gain)
    own_ref[SURE:REST, :] = third[0 : REST - SURE, :]
    trade_ref[0:SURE, :] = flip(normalize(h3[...], gain))
    trade_ref[SURE:REST, :] = flip(third)[0 : REST - SURE, :]

    level = lax.broadcasted_iota(jnp.int32, (NOTES, tgt_lanes), 0)
    source = lax.broadcasted_iota(jnp.int32, (tgt_lanes, TILE), 0)
    lane = lax.broadcasted_iota(jnp.int32, (1, TILE), 1)

    def notes(local, keep):
        block = (
            (local >= SURE).astype(jnp.int32)
            + (local >= 2 * SURE).astype(jnp.int32)
            + (local >= 3 * SURE).astype(jnp.int32)
        )
        at = local + block * ((VOCAB - 1) * SURE) + which[0] * SURE
        at = jnp.where(keep, at, -1)
        found = jnp.zeros((NOTES, TILE), jnp.float32)
        for row in range(tgt_rows):
            wanted = tgt_ref[row : row + 1, :]
            digits = jnp.where(level == 0, wanted & 127, jnp.where(level == 1, wanted >> 7, 0))
            pick = jnp.where(source == at - row * tgt_lanes, 1.0, 0.0).astype(jnp.bfloat16)
            found += jnp.dot(
                digits.astype(jnp.float32).astype(jnp.bfloat16),
                pick,
                preferred_element_type=jnp.float32,
            )
        return found.astype(jnp.bfloat16)

    own_ref[REST : REST + NOTES, :] = jnp.zeros((NOTES, own_ref.shape[1]), jnp.bfloat16)
    own_ref[REST : REST + NOTES, 0:TILE] = notes(lane, lane < EVEN)
    trade_ref[REST : REST + NOTES, :] = jnp.zeros((NOTES, own_ref.shape[1]), jnp.bfloat16)
    trade_ref[REST : REST + NOTES, 0:TILE] = notes(
        2 * EVEN - 1 - lane, (lane >= SURE) & (lane < EVEN)
    )


def prepare(hidden, gain, targets, quarter):
    width = hidden.shape[1]

    def block(j):
        return pl.BlockSpec((SURE, width), lambda i, which, j=j: (VOCAB * j + which[0], 0))

    def whole(*shape):
        return pl.BlockSpec(shape, lambda i, which: (0, 0))

    return pl.pallas_call(
        prep_kernel,
        grid_spec=pltpu.PrefetchScalarGridSpec(
            num_scalar_prefetch=1,
            grid=(1,),
            in_specs=[block(j) for j in range(4)] + [whole(1, width), whole(*targets.shape)],
            out_specs=[whole(n, width) for n in (SURE, REST + NOTES, REST + NOTES)],
        ),
        out_shape=[
            jax.ShapeDtypeStruct((n, width), jnp.bfloat16) for n in (SURE, REST + NOTES, REST + NOTES)
        ],
        cost_estimate=pl.CostEstimate(flops=4 * 10**8, bytes_accessed=3 * 10**6, transcendentals=SHARE),
        name="prep",
    )(quarter.reshape(1), hidden, hidden, hidden, hidden, gain[None, :], targets)


def merge_kernel(live_ref, own_ref, traded_ref, sizes_ref, out_ref):
    live = live_ref[0]
    for low in range(0, REST, 48):
        slot = lax.broadcasted_iota(jnp.int32, (48, own_ref.shape[1]), 0) + (SURE + low)
        out_ref[low : low + 48, :] = jnp.where(
            slot < live,
            own_ref[low : low + 48, :].astype(jnp.float32),
            traded_ref[low : low + 48, :].astype(jnp.float32),
        ).astype(jnp.bfloat16)
    lane = lax.broadcasted_iota(jnp.int32, (NOTES, TILE), 1)
    out_ref[REST : REST + NOTES, :] = jnp.zeros((NOTES, own_ref.shape[1]), jnp.bfloat16)
    out_ref[REST : REST + NOTES, 0:TILE] = (
        jnp.where(
            lane < live,
            own_ref[REST : REST + NOTES, 0:TILE].astype(jnp.float32),
            traded_ref[REST : REST + NOTES, 0:TILE].astype(jnp.float32),
        )
        + sizes_ref[...]
    ).astype(jnp.bfloat16)


def merge(live, own, traded, sizes):
    def whole(array):
        return pl.BlockSpec(array.shape, lambda i, s: (0, 0))

    return pl.pallas_call(
        merge_kernel,
        grid_spec=pltpu.PrefetchScalarGridSpec(
            num_scalar_prefetch=1,
            grid=(1,),
            in_specs=[whole(own), whole(traded), whole(sizes)],
            out_specs=whole(own),
        ),
        out_shape=jax.ShapeDtypeStruct(own.shape, own.dtype),
        cost_estimate=pl.CostEstimate(flops=10**6, bytes_accessed=3 * 10**6, transcendentals=0),
        name="merge",
    )(live.reshape(1), own, traded, sizes)


def stats_kernel(units, n_sets, n_known, final, head_plan, scalars, *refs):
    known_ref = refs[0] if n_known else None
    refs = refs[1:] if n_known else refs
    tok_refs = refs[: 2 * n_sets]
    n_head_refs = 1 + max(index for index, _ in head_plan)
    head_refs = refs[2 * n_sets : 2 * n_sets + n_head_refs]
    (out_ref, tok_buf, head_buf, logit_buf, state, wanted_buf, tok_sem, head_sem) = refs[
        2 * n_sets + n_head_refs :
    ]
    n_groups = len(head_plan) // 2
    n_units = len(units)
    at_set, at_group, at_base = 2, 2 + n_units + 1, 2 + 2 * (n_units + 1)
    z, offset = scalars[0], scalars[1]
    lanes = (8, TILE)

    def fetch(g):
        for piece in (2 * g, 2 * g + 1):
            index, start = head_plan[piece]
            pltpu.make_async_copy(
                head_refs[index].at[pl.ds(start, PIECE)],
                head_buf.at[pl.ds(piece * PIECE, PIECE)],
                head_sem.at[piece],
            ).start()

    def tok_copy(half):
        return pltpu.make_async_copy(
            tok_refs[half],
            tok_buf.at[half // 2, pl.ds(SURE * (half % 2), tok_refs[half].shape[0])],
            tok_sem.at[half],
        )

    for half in range(2 * n_sets):
        tok_copy(half).start()
    for g in range(min(2, n_groups)):
        fetch(g)
    logit_buf[...] = jnp.full(logit_buf.shape, LOW, jnp.float32)
    for k in range(n_sets):
        state[k, 0] = jnp.full(lanes, LOW, jnp.float32)
        for row in range(1, 4):
            state[k, row] = jnp.zeros(lanes, jnp.float32)
    if not final:
        for k in range(n_known):
            for row in range(4):
                state[k, row, 0:1, :] = known_ref[k, row : row + 1, :]
    notes = []
    for k in range(n_sets):
        tok_copy(2 * k).wait()
        tok_copy(2 * k + 1).wait()
        digits = tok_buf[k, EVEN:TILE, 0:TILE].astype(jnp.float32)
        wanted_buf[k] = (digits[0:1, :] + 128.0 * digits[1:2, :]).astype(jnp.int32) - offset
        notes.append(digits[2:3, :] + 128.0 * digits[3:4, :])
    chunk = 64
    rows = lax.broadcasted_iota(jnp.int32, (chunk // 8,) + lanes, 0) * 8 + lax.broadcasted_iota(
        jnp.int32, (chunk // 8,) + lanes, 1
    )

    def part(row):
        return logit_buf[row : row + chunk, :].reshape((chunk // 8,) + lanes)

    def reduce(entry):
        k, g = scalars[at_set + entry], scalars[at_group + entry]
        top_before = state[k, 0]
        top = top_before
        for row in range(0, GROUP, chunk):
            top = jnp.maximum(top, jnp.max(part(row), axis=0))
        shift = top_before - top
        scale = jnp.exp(shift)
        total_before = state[k, 1]
        total = total_before * scale
        moment = (state[k, 2] + shift * total_before) * scale
        picked = state[k, 3]
        for half in range(2):
            wanted = wanted_buf[k] - scalars[at_base + 2 * g + half]
            for row in range(0, PIECE, chunk):
                logits = part(half * PIECE + row)
                under = logits - top[None]
                weight = jnp.exp(under)
                total += jnp.sum(weight, axis=0)
                moment += jnp.sum(weight * under, axis=0)
                picked += jnp.sum(jnp.where(rows == (wanted - row)[None], logits, 0.0), axis=0)
        state[k, 0] = top
        state[k, 1] = total
        state[k, 2] = moment
        state[k, 3] = picked

    def body(u, carry):
        for ahead in range(2, n_groups):

            @pl.when(u + 2 == ahead)
            def _():
                fetch(ahead)

        @pl.when(u < n_groups)
        def _():
            for half in range(2):
                pltpu.make_async_copy(
                    head_refs[0].at[pl.ds(0, PIECE)],
                    head_buf.at[pl.ds(u * GROUP + half * PIECE, PIECE)],
                    head_sem.at[2 * u + half],
                ).wait()

        reduce(u)
        k, g = scalars[at_set + u + 1], scalars[at_group + u + 1]
        logit_buf[...] = lax.dot_general(
            head_buf[pl.ds(pl.multiple_of(g * GROUP, GROUP), GROUP), :],
            tok_buf[k],
            (((1,), (1,)), ((), ())),
            preferred_element_type=jnp.float32,
        )
        return carry

    lax.fori_loop(0, n_units, body, 0)
    reduce(n_units)
    for k in range(n_sets):
        top8 = state[k, 0]
        top = jnp.max(top8, axis=0, keepdims=True)
        shift = top8 - top
        scale = jnp.exp(shift)
        to = out_ref.at[z ^ (NZ - 1)] if final else out_ref.at[k]
        to[0:1, :] = top
        to[1:2, :] = jnp.sum(state[k, 1] * scale, axis=0, keepdims=True)
        to[2:3, :] = jnp.sum((state[k, 2] + shift * state[k, 1]) * scale, axis=0, keepdims=True)
        to[3:4, :] = jnp.sum(state[k, 3], axis=0, keepdims=True)
        to[4:5, :] = notes[k]
        to[5:8, :] = jnp.zeros((3, TILE), jnp.float32)
    if final:
        for k in range(n_known):
            out_ref[z ^ k] = known_ref[k]


def statistics(name, z, offset, sets, heads, plan, known=None, final=False):
    arrays, head_plan = [], []
    for array, start, _ in heads:
        for index, seen in enumerate(arrays):
            if seen is array:
                break
        else:
            index = len(arrays)
            arrays.append(array)
        head_plan.append((index, start))
    n_groups = len(heads) // 2
    units = [(k, g) for k, first, last in plan for g in range(first, last)]
    fixed = [units[0][0]] + [k for k, _ in units] + [n_groups] + [g for _, g in units]
    scalars = jnp.concatenate(
        [
            jnp.stack([z, offset]),
            jnp.array(fixed, jnp.int32),
            jnp.stack([base for _, _, base in heads]),
            jnp.array([1 << 30, 1 << 30], jnp.int32),
        ]
    ).astype(jnp.int32)
    width = arrays[0].shape[1]
    vocab = len(heads) * PIECE
    before = [] if known is None else [known]
    n_known = 0 if known is None else known.shape[0]
    n_out = NZ if final else len(sets)
    pairs = len(units) * GROUP * TILE
    return pl.pallas_call(
        functools.partial(stats_kernel, units, len(sets), n_known, final, head_plan),
        grid_spec=pltpu.PrefetchScalarGridSpec(
            num_scalar_prefetch=1,
            grid=(1,),
            in_specs=[pl.BlockSpec(array.shape, lambda i, s: (0, 0, 0)) for array in before]
            + [pl.BlockSpec(memory_space=pl.ANY)] * (2 * len(sets) + len(arrays)),
            out_specs=pl.BlockSpec((n_out, 8, TILE), lambda i, s: (0, 0, 0)),
            scratch_shapes=[
                pltpu.VMEM((len(sets), TILE, width), jnp.bfloat16),
                pltpu.VMEM((vocab, width), jnp.bfloat16),
                pltpu.VMEM((GROUP, TILE), jnp.float32),
                pltpu.VMEM((len(sets), 4, 8, TILE), jnp.float32),
                pltpu.VMEM((len(sets), 1, TILE), jnp.int32),
                pltpu.SemaphoreType.DMA((2 * len(sets),)),
                pltpu.SemaphoreType.DMA((len(heads),)),
            ],
        ),
        out_shape=jax.ShapeDtypeStruct((n_out, 8, TILE), jnp.float32),
        compiler_params=pltpu.CompilerParams(vmem_limit_bytes=61 * 1024 * 1024),
        cost_estimate=pl.CostEstimate(
            flops=2 * pairs * width,
            bytes_accessed=2 * (len(sets) * TILE + vocab) * width,
            transcendentals=pairs,
        ),
        name=name,
    )(scalars, *before, *[half for pair in sets for half in pair], *arrays)


def after(values, *deps):
    return lax.optimization_barrier((values, deps))[0]


def join(parts):
    top = functools.reduce(jnp.maximum, [part[0] for part in parts])
    total = moment = picked = 0.0
    for part in parts:
        shift = part[0] - top
        scale = jnp.exp(shift)
        total += part[1] * scale
        moment += (part[2] + shift * part[1]) * scale
        picked += part[3]
    return top, total, moment, picked


def on_device(hidden, gain, head, targets, lengths, group_map):
    tok = lax.axis_index("tok")
    vocab = lax.axis_index("vocab")
    z, y = tok // NY, tok % NY
    x, core = vocab // 2, vocab % 2
    upper = z >= NZ // 2
    quarter = jnp.where(upper, VOCAB - 1 - vocab, vocab)

    zs = jnp.arange(NZ)

    sure, rest_own, trade = prepare(hidden, gain, targets.reshape(-1, 128), quarter)
    traded = across(trade, 2)
    sizes_own = after(jnp.concatenate([lengths, group_map[:, 0]]), sure)
    load = jnp.sum(sizes_own[:8])
    block_start = (jnp.arange(4) * VOCAB + quarter) * SURE
    live = jnp.sum(jnp.clip(load - block_start, 0, SURE))
    level = jnp.arange(NOTES)[:, None]
    sizes_own = jnp.pad(sizes_own, (0, TILE - 16))[None, :]
    sizes_own = jnp.where(level == 2, sizes_own & 127, jnp.where(level == 3, sizes_own >> 7, 0))

    rest = merge(live, rest_own, traded, sizes_own.astype(jnp.float32))
    sure_1, sure_2 = across(sure, 1), across(after(sure, traded), 2)
    rest_1, rest_2 = across(rest, 1), across(rest, 2)
    sure_3 = across(sure_2, 1)

    head_later = after(head, sure)
    low_half, high_half = head_later[:PIECE], head_later[PIECE:]
    xa, ya = to_x(low_half), to_y(high_half)
    high_later, low_later = after((high_half, low_half), xa, ya)
    xb, yb = to_x(high_later), to_y(low_later)

    def base(at_y, at_x, at_core, half):
        return ((at_y * 2 + at_x) * 2 + at_core) * GROUP + half * PIECE

    def both_cores(piece, at_y, at_x, half):
        return [
            (piece, 0, base(at_y, at_x, core, half)),
            (to_core(piece), 0, base(at_y, at_x, 1 - core, half)),
        ]

    head_core = to_core(head)
    heads_own = [
        (array, half * PIECE, base(y, x, at_core, half))
        for array, at_core in ((head, core), (head_core, 1 - core))
        for half in range(2)
    ]
    xa_later, ya_later = after((xa, ya), traded)
    heads = heads_own + both_cores(xa_later, y, 1 - x, 0) + both_cores(ya_later, 1 - y, x, 1)
    offset = z * (TOK * VOCAB // NZ * head.shape[0])
    run = functools.partial(statistics, z=z, offset=offset)

    x2, y2 = to_x(after(ya, xb, yb)), to_y(after(xa, xb, yb))
    heads = heads + both_cores(xb, y, 1 - x, 1) + both_cores(yb, 1 - y, x, 0)
    early = run(
        "first",
        sets=[(sure, rest), (sure_1, rest_1)],
        heads=heads,
        plan=[(0, 0, 6), (1, 0, 6)],
    )
    rest_2, sure_3, x2, y2 = after((rest_2, sure_3, x2, y2), early)
    rest_3 = across(rest_2, 1)
    heads = heads + both_cores(x2, 1 - y, 1 - x, 1) + both_cores(y2, 1 - y, 1 - x, 0)
    early = run(
        "second",
        sets=[(sure, rest), (sure_1, rest_1), (sure_2, rest_2)],
        heads=heads,
        plan=[(2, 0, 8), (0, 6, 8), (1, 6, 8)],
        known=early,
    )
    rest_3 = after(rest_3, early)
    own_stats = run(
        "third", sets=[(sure_3, rest_3)], heads=heads, plan=[(0, 0, 8)], known=early, final=True
    )

    parts = [own_stats] + [across(own_stats, step) for step in (1, 2, 3)]
    top, total, moment, picked = join([jnp.moveaxis(part[:, :4, :EVEN], 1, 0) for part in parts])
    spread = jnp.log(total)
    logprob = picked - top - spread
    entropy = spread - moment / total
    partner = jnp.array([2, 3, 0, 1])
    sizes = own_stats[:, 4, :16].astype(jnp.int32)
    own_lengths = sizes[:, :8]
    loads = jnp.sum(own_lengths, axis=1)
    quarters = jnp.where(zs >= NZ // 2, VOCAB - 1 - vocab, vocab)
    starts_of = (jnp.arange(4)[None, :] * VOCAB + quarters[:, None]) * SURE
    lives = jnp.sum(jnp.clip(loads[:, None] - starts_of, 0, SURE), axis=1)
    slots = jnp.arange(EVEN)
    stays = slots[None, :] < lives[:, None]

    local = jnp.where(stays, slots[None, :], 2 * EVEN - 1 - slots[None, :])
    origin = jnp.where(stays, zs[:, None], partner[:, None])
    origin_quarter = jnp.where(origin >= NZ // 2, VOCAB - 1 - vocab, vocab)
    row = (local // SURE * VOCAB + origin_quarter) * SURE + local % SURE
    place = origin * hidden.shape[0] + row
    finish = jnp.cumsum(own_lengths, axis=1) + zs[:, None] * hidden.shape[0]
    begin = finish - own_lengths
    member = (place[:, :, None, None] >= begin) & (place[:, :, None, None] < finish)
    sums_part = jnp.sum(jnp.where(member, logprob[:, :, None, None], 0.0), axis=(0, 1))

    results = jnp.stack([logprob, entropy])
    mine = lax.dynamic_index_in_dim(results, z, 1, False)
    theirs = lax.dynamic_index_in_dim(results, z ^ 2, 1, False)
    local_rows = jnp.concatenate([mine, jnp.flip(theirs[:, SURE:], 1)], 1)
    local_rows = jnp.where(jnp.arange(SHARE)[None, :] < live, local_rows, 0.0)
    gathered = lax.all_gather(
        jnp.concatenate([local_rows.reshape(1, -1), sums_part.reshape(1, -1)], 1), "vocab"
    ).reshape(VOCAB, -1)
    sums_own = jnp.concatenate(
        [
            jnp.sum(gathered[:, 2 * SHARE :], axis=0).reshape(NZ, 8),
            sizes.astype(jnp.float32),
        ],
        1,
    )
    sums_other = to_y(sums_own)
    sums = jnp.where(
        y == 0, jnp.stack([sums_own, sums_other], 1), jnp.stack([sums_other, sums_own], 1)
    )
    all_lengths, all_groups = sums[:, :, 8:16], sums[:, :, 16:].astype(jnp.int32)
    sums = sums[:, :, :8]
    parts = gathered[:, : 2 * SHARE].reshape(VOCAB, 2, SHARE)
    parts = lax.dynamic_slice_in_dim(parts, vocab * SURE, SURE, 2)
    parts = jnp.where(upper, jnp.flip(parts, 0), parts)
    out = parts.transpose(1, 0, 2).reshape(2, SHARE)

    means = (sums / all_lengths).reshape(-1)
    onehot = (
        all_groups.reshape(-1)[:, None] == jnp.arange(TOK, dtype=jnp.int32)[None, :]
    ).astype(jnp.float32)
    group_mean = jnp.sum(onehot * means[:, None], axis=0) / jnp.sum(onehot, axis=0)
    centered = means - jnp.sum(onehot * group_mean[None, :], axis=1)
    return out[0], out[1], lax.dynamic_slice_in_dim(centered, tok * 8 + vocab * 2, 2, 0)


def solution(mesh):
    fits = mesh.shape["tok"] == TOK and mesh.shape["vocab"] == VOCAB
    return jax.shard_map(
        on_device if fits else on_any_mesh,
        mesh=mesh,
        in_specs=(
            P("tok", None),
            P(),
            P(("tok", "vocab"), None),
            P("tok"),
            P("tok"),
            P("tok", None),
        ),
        out_specs=(P(("tok", "vocab")), P(("tok", "vocab")), P(("tok", "vocab"))),
        check_vma=False,
    )
```
